32 devices in a mesh: grp: 2 (over y), seq: 8 (over z, x), chan: 2 (over core).
Axes of the slice: x: 2, y: 2, z: 4, core: 2. Of those that a mesh axis runs over, the one named last changes fastest.
Arguments:
- streams: bfloat16 [3, 2048, 2048], P(None, 'chan', ('grp', 'seq')), parts along dimension 2, may hold values from -6 to 6
- short_weight: float32 [3, 7, 2048], P(None, None, 'chan'), may hold values from -2 to 2
- filter_modes: int32 [16], replicated, may hold values from 1 to 511
- filter_first: float32 [32, 64], replicated, may hold values from -6 to 6
- filter_out: float32 [64, 2048], P(None, 'chan'), may hold values from -0.75 to 0.75
- decay_rate: float32 [2048], P('chan'), may hold values from 1e-05 to 0.05
- skip_gain: float32 [2048], P('chan'), may hold values from -1 to 1
- w_out: bfloat16 [2048, 2048], P('chan', 'seq'), may hold values from -0.1875 to 0.1875
Outputs:
- mixed_out: bfloat16 [2048, 2048], P(('grp', 'seq'), 'chan'), parts along dimension 0
The draws below stay inside these ranges and needn't reach their ends.
There are 2 independent parts, one for each index of `grp`. The reference program is written for one: setup_inputs(seed, part) draws one part's arguments, and reference() takes and returns one part's arrays. A program takes and returns all parts, laid end to end along the dimension named above; an argument that names none is the same for every part. Nothing has to cross between parts.
All inputs are finite; a program needn't handle non-finite values.
Results may differ from the reference program's by a relative error of at most 0.013.
Values may be sent and summed in bfloat16 or wider, within the bound.
A program may use at most 64 MiB of HBM per device.

```python
import math
import jax
import jax.numpy as jnp
from jax import lax

D_CH = 2048
D_OUT = 2048
FH = 64
BANDS = 16
TAPS = 7
T_DEV = 128
SEQ_LEN = 1024
N_SEQ = 8


def touch_ends(values, own_key, least, top_value):
    spot = [jax.random.randint(jax.random.fold_in(own_key, axis), (), 0, length) for axis, length in enumerate(values.shape)]
    longest = values.shape.index(max(values.shape))
    beside = spot[:longest] + [(spot[longest] + 1) % values.shape[longest]] + spot[longest + 1:]
    return values.at[tuple(spot)].set(least).at[tuple(beside)].set(top_value)


def raised(drawn, rng, source, target, shards_of, factor):
    def block_of(axis_at):
        return (jnp.arange(drawn.shape[axis_at]) // (drawn.shape[axis_at] // shards_of)).reshape((-1,) + (1,) * (drawn.ndim - 1 - axis_at))

    near = jax.random.permutation(rng, shards_of)[block_of(target)]
    second = (block_of(target) + shards_of // 2) % shards_of
    return jnp.where((block_of(source) == near) | (block_of(source) == second), factor * drawn, drawn)


def levels(stream_key, dims, cuts, smallest, high):
    def one(dim, blocks):
        heights = jax.random.uniform(jax.random.fold_in(jax.random.fold_in(stream_key, 6), dim), (blocks,), jnp.float32, smallest / len(cuts), high / len(cuts))
        return jnp.repeat(jnp.exp(heights), dims[dim] // blocks).reshape((-1,) + (1,) * (len(dims) - dim - 1))

    gain = one(*cuts[0])
    for cut in cuts[1:]:
        gain = gain * one(*cut)
    return gain


def normal_values(own_key, shape, deviation, most, shards=(), kind=jnp.bfloat16):
    values = deviation * jax.random.normal(own_key, shape, jnp.float32)
    if shards:
        values = values * levels(own_key, shape, shards, -0.22, 0.18)
    return jnp.clip(values, -most, most).astype(kind)


def noise_with(own_key, shape, width, most, split, heavy, kind=jnp.bfloat16):
    values = width * jax.random.normal(own_key, shape, jnp.float32)
    if split:
        values = values * levels(own_key, shape, split, -0.22, 0.18)
    return jnp.clip(raised(values, jax.random.fold_in(own_key, 3), *heavy), -most, most).astype(kind)


def setup_inputs(seed: int = 0, part: int = 0) -> dict:
    arg_keys = jax.random.split(jax.random.key(seed), 9)
    part_keys = jax.random.split(jax.random.fold_in(arg_keys[8], part), 9)
    return {
        "streams": normal_values(part_keys[0], (3, D_CH, SEQ_LEN), 1.0, 6.0, ((1, 2), (2, 8))),
        "short_weight": normal_values(arg_keys[1], (3, TAPS, D_CH), TAPS ** -0.5, 2.0, ((2, 2),), jnp.float32),
        "filter_modes": touch_ends(jax.random.randint(arg_keys[2], (BANDS,), 1, SEQ_LEN // 2), jax.random.fold_in(arg_keys[2], 1), 1, (SEQ_LEN // 2) - 1).astype(jnp.int32),
        "filter_first": normal_values(arg_keys[3], (2 * BANDS, FH), 1.0, 6.0, (), jnp.float32),
        "filter_out": normal_values(arg_keys[4], (FH, D_CH), FH ** -0.5, 0.75, ((1, 2),), jnp.float32),
        "decay_rate": jnp.clip(jnp.exp(math.log(0.05) - 8.517193 * jax.random.uniform(arg_keys[5], (D_CH,), jnp.float32) ** levels(arg_keys[5], (D_CH,), ((0, 2),), -0.2, 0.2)), 9.999999747378752e-06, 0.05),
        "skip_gain": jnp.clip(jax.random.uniform(arg_keys[6], (D_CH,), jnp.float32, -1.0, 1.0) * levels(arg_keys[6], (D_CH,), ((0, 2),), -0.4, 0.0), -1.0, 1.0),
        "w_out": noise_with(arg_keys[7], (D_CH, D_OUT), D_CH ** -0.5, 0.1875, ((0, 2), (1, 8)), (0, 1, 8, 2.0)),
    }


def position_filter(positions, mode_ints, first_layer, out_cols, decay_rates, tokens_dev, seq_count):
    total_len = tokens_dev * seq_count
    block_idx = positions // tokens_dev
    offset_idx = positions % tokens_dev
    upper_part = mode_ints[:, None] * block_idx[None, :] % seq_count
    lower_part = mode_ints[:, None] * offset_idx[None, :] % total_len
    phase_int = ((tokens_dev * upper_part + lower_part) % total_len).astype(jnp.int32)
    phase_angle = phase_int.astype(jnp.float32) * jnp.float32(2.0 * math.pi / total_len)
    features = jnp.concatenate([jnp.cos(phase_angle), jnp.sin(phase_angle)], axis=0)
    hidden = jnp.sin(jnp.dot(first_layer.T, features, precision=lax.Precision.HIGHEST, preferred_element_type=jnp.float32))
    raw_values = jnp.dot(out_cols.T, hidden, precision=lax.Precision.HIGHEST, preferred_element_type=jnp.float32)
    time_float = positions.astype(jnp.float32)
    scaled = jnp.sqrt(2.0 * decay_rates)[:, None] * jnp.exp(-decay_rates[:, None] * time_float[None, :]) * raw_values
    return scaled.astype(jnp.bfloat16)

def causal_block(pair_block):
    signal_blk, filter_blk = pair_block
    length = signal_blk.shape[1]
    spectrum = jnp.fft.rfft(signal_blk, n=2 * length, axis=1) * jnp.fft.rfft(filter_blk, n=2 * length, axis=1)
    return jnp.fft.irfft(spectrum, n=2 * length, axis=1)[:, :length]

def reference(streams, short_weight, filter_modes, filter_first, filter_out, decay_rate, skip_gain, w_out):
    reach = TAPS - 1
    padded = jnp.pad(streams.astype(jnp.float32), ((0, 0), (0, 0), (reach, 0)))
    feature = short_weight[:, 0, :, None] * padded[:, :, reach:]
    for tap_index in range(1, TAPS):
        feature = feature + short_weight[:, tap_index, :, None] * padded[:, :, reach - tap_index:reach - tap_index + SEQ_LEN]
    query = feature[0].astype(jnp.bfloat16)
    kv_product = (feature[1] * feature[2]).astype(jnp.bfloat16)
    positions = jnp.arange(SEQ_LEN, dtype=jnp.int32)
    long_filter = position_filter(positions, filter_modes, filter_first, filter_out, decay_rate, T_DEV, N_SEQ)
    block_rows = 128
    count_blocks = D_CH // block_rows
    signal_all = kv_product.astype(jnp.float32).reshape(count_blocks, block_rows, SEQ_LEN)
    filter_all = long_filter.astype(jnp.float32).reshape(count_blocks, block_rows, SEQ_LEN)
    conv = lax.map(causal_block, (signal_all, filter_all)).reshape(D_CH, SEQ_LEN).astype(jnp.bfloat16)
    gated = (query.astype(jnp.float32) * (conv.astype(jnp.float32) + skip_gain[:, None] * kv_product.astype(jnp.float32))).astype(jnp.bfloat16)
    mixed = lax.dot_general(gated, w_out, (((0,), (0,)), ((), ())), preferred_element_type=jnp.float32)
    return mixed.astype(jnp.bfloat16)
```

```python
import functools
import math

import jax
import jax.numpy as jnp
import numpy as np
from jax import lax
from jax.experimental import pallas as pl
from jax.experimental.pallas import tpu as pltpu
from jax.sharding import PartitionSpec as P


def shifted(value, axis, steps):
    count = lax.axis_size(axis)
    leading, last = (max(0, -steps), min(count, count - steps))
    return lax.ppermute(value, axis, [(source, source + steps) for source in range(leading, last)])


def position_filter(
    positions, mode_ints, first_layer, out_cols, decay_rates, tokens_dev, seq_count
):
    total_len = tokens_dev * seq_count
    block_idx = positions // tokens_dev
    offset_idx = positions % tokens_dev
    upper_part = mode_ints[:, None] * block_idx[None, :] % seq_count
    lower_part = mode_ints[:, None] * offset_idx[None, :] % total_len
    phase_int = (tokens_dev * upper_part + lower_part) % total_len
    phase_angle = phase_int.astype(jnp.float32) * jnp.float32(2.0 * math.pi / total_len)
    features = jnp.concatenate([jnp.cos(phase_angle), jnp.sin(phase_angle)], axis=0)
    hidden = jnp.sin(
        jnp.dot(
            first_layer.T,
            features,
            precision=lax.Precision.HIGHEST,
            preferred_element_type=jnp.float32,
        )
    )
    raw_values = jnp.dot(
        out_cols.T, hidden, precision=lax.Precision.HIGHEST, preferred_element_type=jnp.float32
    )
    time_float = positions.astype(jnp.float32)
    scaled = (
        jnp.sqrt(2.0 * decay_rates)[:, None]
        * jnp.exp(-decay_rates[:, None] * time_float[None, :])
        * raw_values
    )
    return scaled.astype(jnp.bfloat16)


def angle_table(rows_count, cols_count, modulus):
    product = (
        jnp.arange(rows_count, dtype=jnp.int32)[:, None]
        * jnp.arange(cols_count, dtype=jnp.int32)[None, :]
        % modulus
    )
    phase_angle = product.astype(jnp.float32) * jnp.float32(2.0 * math.pi / modulus)
    return (jnp.cos(phase_angle), jnp.sin(phase_angle))


def contract(form, left, right):
    return jnp.einsum(
        form, left, right, precision=lax.Precision.HIGHEST, preferred_element_type=jnp.float32
    )


def local(
    streams, short_weight, filter_modes, filter_first, filter_out, decay_rate, skip_gain, w_out
):
    seq_count = lax.axis_size("seq")
    seq_index = lax.axis_index("seq")
    width_half = streams.shape[1]
    tokens_dev = streams.shape[2]
    reach = short_weight.shape[1] - 1
    per_device = width_half // seq_count
    total_len = tokens_dev * seq_count
    rim = shifted(streams[:, :, tokens_dev - reach :], "seq", 1)
    extended = jnp.concatenate([rim, streams], axis=2).astype(jnp.float32)
    feature = short_weight[:, 0, :, None] * extended[:, :, reach:]
    for tap_index in range(1, reach + 1):
        feature = (
            feature
            + short_weight[:, tap_index, :, None]
            * extended[:, :, reach - tap_index : reach - tap_index + tokens_dev]
        )
    query = feature[0].astype(jnp.bfloat16)
    kv_product = (feature[1] * feature[2]).astype(jnp.bfloat16)
    positions = seq_index * tokens_dev + jnp.arange(tokens_dev, dtype=jnp.int32)
    filter_local = position_filter(
        positions, filter_modes, filter_first, filter_out, decay_rate, tokens_dev, seq_count
    )
    kv_channels, filter_channels = (
        lax.all_to_all(kv_product, "seq", split_axis=0, concat_axis=1, tiled=True),
        lax.all_to_all(filter_local, "seq", split_axis=0, concat_axis=1, tiled=True),
    )
    doubled = 2 * seq_count
    padded_len = 2 * total_len
    cos_outer, sin_outer = angle_table(doubled, seq_count, doubled)
    cos_twist, sin_twist = angle_table(doubled, tokens_dev, padded_len)
    cos_inner, sin_inner = angle_table(tokens_dev, tokens_dev, tokens_dev)

    def forward(signal):
        shaped = signal.astype(jnp.float32).reshape(per_device, seq_count, tokens_dev)
        a_real = contract("cpj,kp->ckj", shaped, cos_outer)
        a_imag = -contract("cpj,kp->ckj", shaped, sin_outer)
        r_real = a_real * cos_twist + a_imag * sin_twist
        r_imag = a_imag * cos_twist - a_real * sin_twist
        x_real = contract("ckj,jm->ckm", r_real, cos_inner) + contract(
            "ckj,jm->ckm", r_imag, sin_inner
        )
        x_imag = contract("ckj,jm->ckm", r_imag, cos_inner) - contract(
            "ckj,jm->ckm", r_real, sin_inner
        )
        return (x_real, x_imag)

    kv_real, kv_imag = forward(kv_channels)
    fl_real, fl_imag = forward(filter_channels)
    y_real = kv_real * fl_real - kv_imag * fl_imag
    y_imag = kv_real * fl_imag + kv_imag * fl_real
    b_real = contract("ckm,mj->ckj", y_real, cos_inner) - contract("ckm,mj->ckj", y_imag, sin_inner)
    b_imag = contract("ckm,mj->ckj", y_imag, cos_inner) + contract("ckm,mj->ckj", y_real, sin_inner)
    t_real = b_real * cos_twist - b_imag * sin_twist
    t_imag = b_real * sin_twist + b_imag * cos_twist
    conv_values = contract("ckj,kp->cpj", t_real, cos_outer) - contract(
        "ckj,kp->cpj", t_imag, sin_outer
    )
    conv_channels = (
        (conv_values * jnp.float32(1.0 / padded_len))
        .reshape(per_device, total_len)
        .astype(jnp.bfloat16)
    )
    conv_tokens = lax.all_to_all(conv_channels, "seq", split_axis=1, concat_axis=0, tiled=True)
    gated = (
        query.astype(jnp.float32)
        * (conv_tokens.astype(jnp.float32) + skip_gain[:, None] * kv_product.astype(jnp.float32))
    ).astype(jnp.bfloat16)
    partial_out = lax.dot_general(
        gated,
        lax.all_gather(w_out, "seq", axis=1, tiled=True),
        (((0,), (0,)), ((), ())),
        preferred_element_type=jnp.float32,
    )
    return lax.psum_scatter(partial_out, "chan", scatter_dimension=1, tiled=True).astype(
        jnp.bfloat16
    )


LANES = 128
CHUNKS = 4
QLAG = 7
GLAG = 3
PLAN = {'kv': ('x0', 'x1', 'x2', 'x3'), 'top': (), 'q': ((), (), (), (), (), (), ('z0', 'z1', 'z2', 'z3', 'X0', 'X1', 'X2', 'X3')), 'land': ('Z0', 'Z1'), 'conv': ('Z2', 'Z3', 'D0'), 'g0': ('D1', 'D2'), 'g1': ((), (), (), ('D3',), (), (), ()), 'far': ((), (), (), ())}
MESH = pl.DeviceIdType.MESH


def tables(block):
    size = 2 * block
    steps = np.arange(size)
    angle = 2.0 * np.pi * (np.outer(np.arange(block), steps) % size) / size
    forward = np.concatenate([np.cos(angle), -np.sin(angle)], axis=0)
    forward[block] = np.cos(np.pi * steps)
    weight = np.full((size, 1), 2.0 / size)
    weight[0] = weight[block] = 1.0 / size
    inverse = (forward * weight).T[block:]
    upper = np.asarray(forward, dtype=jnp.bfloat16)
    lower = np.asarray(forward - upper.astype(np.float64), dtype=jnp.bfloat16)
    both = np.concatenate([upper[:, :block], lower[:, :block]], axis=1)
    unit = np.eye(block, size)
    return np.concatenate(
        [upper, lower, both, np.asarray(inverse, jnp.bfloat16), np.asarray(unit, jnp.bfloat16)], axis=0
    )


def split_pi():
    parts, rest = [], math.pi
    for bits in (10, 22):
        part = math.floor(rest * 2.0**bits) / 2.0**bits
        parts.append(part)
        rest -= part
    return (*parts, rest)


def sine(value):
    f32 = jnp.float32
    count = jnp.floor(value * f32(1.0 / math.pi) + f32(0.5))
    rest = value
    for part in split_pi():
        rest = rest - count * f32(part)
    half = count * f32(0.5)
    sign = f32(1.0) - f32(4.0) * (half - jnp.floor(half))
    square = rest * rest
    series = f32(0.0)
    for degree in range(13, 1, -2):
        series = (series + f32((-1.0) ** (degree // 2) / math.factorial(degree))) * square
    return sign * (rest + rest * series)


def mixer(
    seq_count, streams_h, short_h, modes_h, first_h, filter_h, decay_h, skip_h, w_h, table_h, out,
    streams, short_weight, modes, first, filter_cols, decay, skip, w_out, table,
    xt, rim_out, rim_in, kv_own, q_own, kv_all, q_all, spec_x, spec_r, spec_i, spec_n, spec_y,
    gate_own, gate_all, w_next, acc, acc_in, part,
    sem_in, sem_rim, sem_kvm_s, sem_kvm_r, sem_kvh_s, sem_kvh_r, sem_q_s, sem_q_r, sem_g_s, sem_g_r,
    sem_w_s, sem_w_r, sem_a_s, sem_a_r, sem_o_s, sem_o_r,
):
    f32, bf16 = jnp.float32, jnp.bfloat16
    blk = streams.shape[2]
    size = 2 * blk
    taps = short_weight.shape[1]
    total = seq_count * blk
    cols = w_out.shape[1]
    zn = seq_count // 2
    groups = seq_count // 2
    grp = lax.axis_index("grp")
    me = lax.axis_index("seq")
    core = lax.axis_index("chan")
    other = 1 - core
    z = me // 2
    x = me % 2
    side = me // groups
    group = me % groups

    def dev(seq, chan):
        return (grp, seq, chan)

    def lane(i, n=LANES):
        return pl.ds(pl.multiple_of(i * n, n), n)

    barrier = pltpu.get_barrier_semaphore()
    for d in range(1, seq_count):
        for ch in (core, other):
            pl.semaphore_signal(barrier, inc=1, device_id=dev((me + d) % seq_count, ch), device_id_type=MESH)
    for near in (dev(me, other), (1 - grp, me, core)):
        pl.semaphore_signal(barrier, inc=1, device_id=near, device_id_type=MESH)

    here = lane(me)
    loads = (
        (table_h, table),
        (streams_h.at[0], streams.at[0]),
        (streams_h.at[1], streams.at[1]),
        (streams_h.at[2], streams.at[2]),
        (short_h, short_weight),
        (modes_h, modes),
        (first_h, first),
        (filter_h.at[:, here], filter_cols),
        (decay_h.at[:, here], decay),
        (skip_h.at[:, here], skip),
        (w_h, w_out),
    )

    def load(i):
        return pltpu.make_async_copy(loads[i][0], loads[i][1], sem_in.at[i])

    for i in range(len(loads)):
        load(i).start()
    load(0).wait()
    eye = table[4 * blk + 2 * blk + blk : 4 * blk + 2 * blk + 2 * blk, :blk]
    for st in range(3):
        load(1 + st).wait()
        turned = lax.dot_general(eye, streams[st], (((1,), (1,)), ((), ())), preferred_element_type=f32)
        xt[st, 8:, :] = turned
    rim_out[...] = jnp.concatenate([xt[st, blk:, :] for st in range(3)], axis=0).astype(bf16)

    def features(rows):
        def body(l, carry):
            ln = lane(l)
            for r0 in rows:
                feat = []
                for st in range(3):
                    total_f = short_weight[st, pl.ds(0, 1), ln] * xt[st, pl.ds(8 + r0, 16), ln]
                    for i in range(1, taps):
                        total_f = total_f + short_weight[st, pl.ds(i, 1), ln] * xt[st, pl.ds(8 + r0 - i, 16), ln]
                    feat.append(total_f)
                q_own[pl.ds(r0, 16), ln] = feat[0].astype(bf16)
                kv_own[pl.ds(r0, 16), ln] = (feat[1] * feat[2]).astype(bf16)
            return carry

        lax.fori_loop(0, seq_count, body, 0)

    load(4).wait()
    features(range(16, blk, 16))

    pl.semaphore_wait(barrier, 2 * seq_count)

    def rim_copy():
        return pltpu.make_async_remote_copy(
            src_ref=rim_out, dst_ref=rim_in, send_sem=sem_rim.at[0], recv_sem=sem_rim.at[1],
            device_id=dev((me + 1) % seq_count, core), device_id_type=MESH)

    def spread(own, every, send, recv, d, rows):
        to = (me + d) % seq_count
        return pltpu.make_async_remote_copy(
            src_ref=own.at[rows, lane(to)], dst_ref=every.at[rows, lane(me)],
            send_sem=send.at[d], recv_sem=recv.at[d], device_id=dev(to, core), device_id_type=MESH)

    def landing(own, every, send, recv, d, rows):
        source = (me + seq_count - d) % seq_count
        return pltpu.make_async_remote_copy(
            src_ref=own.at[rows, lane(source)], dst_ref=every.at[rows, lane(source)],
            send_sem=send.at[d], recv_sem=recv.at[d], device_id=dev(source, core), device_id_type=MESH)

    main, top, whole = pl.ds(16, blk - 16), pl.ds(0, 16), pl.ds(0, blk)
    order = (4, 3, 5, 2, 6, 1, 7) if seq_count == 8 else tuple(range(1, seq_count))

    @pl.when(me < seq_count - 1)
    def _():
        rim_copy().start()

    for d in order:
        spread(kv_own, kv_all, sem_kvm_s, sem_kvm_r, d, main).start()

    part_rows = w_out.shape[0] // 2
    step_rows = part_rows // CHUNKS
    beside = dev(me + 1 - 2 * x, core)
    above = dev(me + 2 - 4 * (z % 2), core)
    across = (1 - grp, me, core)
    w_source = (w_h, w_h, w_next.at[1], w_next.at[0], w_next.at[1], w_next.at[2])
    w_slot = (0, 1, 2, 0, 1, 2)
    w_to = (beside, above, beside, across, across, across)

    def chunk(side_y, k):
        return pl.ds(pl.multiple_of(side_y * part_rows + k * step_rows, step_rows), step_rows)

    def w_copy(i, k):
        return pltpu.make_async_remote_copy(
            src_ref=w_source[i].at[chunk(grp, k), :], dst_ref=w_next.at[w_slot[i], chunk(grp, k), :],
            send_sem=sem_w_s.at[i, k], recv_sem=sem_w_r.at[i, k], device_id=w_to[i], device_id_type=MESH)

    def w_back(slot, k):
        return pltpu.make_async_remote_copy(
            src_ref=w_next.at[slot, chunk(1 - grp, k), :], dst_ref=w_next.at[slot, chunk(1 - grp, k), :],
            send_sem=sem_w_s.at[3 + slot, k], recv_sem=sem_w_r.at[3 + slot, k], device_id=across, device_id_type=MESH)

    def forward(i, k):
        w_copy(i, k).wait_recv()
        for nxt in ((3,), (4, 2), (5,))[i]:
            w_copy(nxt, k).start()

    def w_steps(*names):
        for name in names:
            i, k = "xzdXZD".index(name[0]), int(name[1:])
            if i < 3:
                w_copy(i, k).start()
            else:
                forward(i - 3, k)

    w_steps(*PLAN["kv"])

    load(5).wait()
    bands = modes.shape[0]
    band = lax.broadcasted_iota(jnp.int32, (bands, LANES), 0)
    mode = jnp.zeros((bands, LANES), jnp.int32)
    for b in range(bands):
        mode = jnp.where(band == b, modes[b], mode)
    mode = jnp.concatenate([mode] * (total // LANES), axis=1)
    steps = lax.broadcasted_iota(jnp.int32, (bands, total), 1)
    phase = (mode * steps) & (total - 1)
    turn_unit = f32(2.0 * math.pi / total)
    positional = sine(jnp.concatenate([phase + total // 4, phase], axis=0).astype(f32) * turn_unit)
    load(6).wait()
    hidden = sine(lax.dot_general(
        first[...], positional, (((0,), (0,)), ((), ())), precision=lax.Precision.HIGHEST,
        preferred_element_type=f32))
    load(7).wait()
    raw = lax.dot_general(
        hidden, filter_cols[...], (((0,), (0,)), ((), ())), precision=lax.Precision.HIGHEST,
        preferred_element_type=f32)
    load(8).wait()
    rate = decay[...]
    root = jnp.sqrt(2.0 * rate)
    pieces = []
    for r in range(seq_count):
        time = (lax.broadcasted_iota(jnp.int32, (blk, LANES), 0) + r * blk).astype(f32)
        pieces.append((root * jnp.exp(-rate * time) * raw[r * blk : (r + 1) * blk]).astype(bf16))
    now = jnp.concatenate(pieces, axis=1)
    before = jnp.concatenate([jnp.zeros((blk, LANES), bf16)] + pieces[:-1], axis=1)
    window = jnp.concatenate([before, now], axis=0)
    spectrum = jnp.dot(table[:size, :], window, preferred_element_type=f32) + jnp.dot(
        table[size : 2 * size, :], window, preferred_element_type=f32)
    row0 = lax.broadcasted_iota(jnp.int32, (blk, total), 0) == 0
    real, imag = spectrum[:blk], spectrum[blk:]
    spec_r[...] = real
    spec_i[...] = jnp.where(row0, 0.0, imag)
    spec_n[...] = jnp.where(row0, imag, real)

    @pl.when(me > 0)
    def _():
        rim_copy().wait_recv()
        for st in range(3):
            xt[st, 0:8, :] = rim_in[8 * st : 8 * st + 8, :].astype(f32)

    @pl.when(me == 0)
    def _():
        for st in range(3):
            xt[st, 0:8, :] = jnp.zeros((8, xt.shape[2]), f32)

    features((0,))
    for d in order:
        spread(kv_own, kv_all, sem_kvh_s, sem_kvh_r, d, top).start()
    w_steps(*PLAN["top"])
    for i, d in enumerate(order):
        if i >= QLAG:
            spread(kv_own, kv_all, sem_kvm_s, sem_kvm_r, order[i - QLAG], main).wait_send()
        spread(q_own, q_all, sem_q_s, sem_q_r, d, whole).start()
        w_steps(*PLAN["q"][i])
    kv_all[:, lane(me)] = kv_own[:, lane(me)]
    q_all[:, lane(me)] = q_own[:, lane(me)]

    for d in order:
        landing(kv_own, kv_all, sem_kvm_s, sem_kvm_r, d, main).wait_recv()
    for d in order:
        landing(kv_own, kv_all, sem_kvh_s, sem_kvh_r, d, top).wait_recv()
    w_steps(*PLAN["land"])
    kv = kv_all[...]
    spec_x[...] = jnp.dot(
        table[2 * size : 3 * size, :], jnp.concatenate([kv, kv], axis=0), preferred_element_type=f32)

    def product(i, carry):
        lo = pl.ds(pl.multiple_of(i * 16, 16), 16)
        hi = pl.ds(pl.multiple_of(blk + i * 16, 16), 16)
        for p in range(seq_count):
            y_real = y_imag = None
            for s in range(p + 1):
                sl, fl = pl.ds(s * LANES, LANES), pl.ds((p - s) * LANES, LANES)
                xr, xi = spec_x[lo, sl], spec_x[hi, sl]
                hr, him, hn = spec_r[lo, fl], spec_i[lo, fl], spec_n[lo, fl]
                tr = xr * hr - xi * him
                ti = xr * him + xi * hn
                y_real = tr if y_real is None else y_real + tr
                y_imag = ti if y_imag is None else y_imag + ti
            spec_y[lo, pl.ds(p * LANES, LANES)] = y_real.astype(bf16)
            spec_y[hi, pl.ds(p * LANES, LANES)] = y_imag.astype(bf16)
        return carry

    lax.fori_loop(0, blk // 16, product, 0)
    conv = jnp.dot(table[3 * size : 3 * size + blk, :], spec_y[...], preferred_element_type=f32)
    w_steps(*PLAN["conv"])
    for d in order:
        landing(q_own, q_all, sem_q_s, sem_q_r, d, whole).wait_recv()
    load(9).wait()
    gain = skip[...]
    for p in range(seq_count):
        sl = pl.ds(p * LANES, LANES)
        inner = conv[:, p * LANES : (p + 1) * LANES].astype(bf16).astype(f32) + gain * kv_all[:, sl].astype(f32)
        gate_own[p % groups, pl.ds((p // groups) * blk, blk), :] = (q_all[:, sl].astype(f32) * inner).astype(bf16)

    def rows_of(j):
        return pl.ds(pl.multiple_of(j * blk, blk), blk)

    def g_send(turn, d):
        to = (me + d) % seq_count
        far = to // groups
        rows = rows_of(1 - far if turn == 0 else far)
        return pltpu.make_async_remote_copy(
            src_ref=gate_own.at[to % groups, rows, :], dst_ref=gate_all.at[z, rows, lane(x)],
            send_sem=sem_g_s.at[turn, d], recv_sem=sem_g_r.at[turn, d], device_id=dev(to, core), device_id_type=MESH)

    def g_land(turn, d):
        source = (me + seq_count - d) % seq_count
        rows = rows_of(1 - side if turn == 0 else side)
        return pltpu.make_async_remote_copy(
            src_ref=gate_own.at[0, rows, :], dst_ref=gate_all.at[source // 2, rows, lane(source % 2)],
            send_sem=sem_g_s.at[turn, d], recv_sem=sem_g_r.at[turn, d], device_id=dev(source, core),
            device_id_type=MESH)

    for d in order:
        g_send(0, d).start()
    gate_all[z, :, lane(x)] = gate_own[group]
    w_steps(*PLAN["g0"])
    for i, d in enumerate(order):
        if i >= GLAG:
            g_send(0, order[i - GLAG]).wait_send()
        g_send(1, d).start()
        w_steps(*PLAN["g1"][i])
    load(10).wait()

    flip_x, flip_z = 1 - 2 * x, 2 - 4 * (z % 2)
    places = (group, group + flip_z, group + flip_x, group + flip_x + flip_z)
    slots = (None, 1, 0, 2)

    def project(j, first_turn, then):
        left = [gate_all[k, rows_of(j), :] for k in range(zn)]
        for i, (place, slot) in enumerate(zip(places, slots)):
            if first_turn:
                w_steps(*PLAN["far"][i])
            if slot is not None and first_turn:
                for k in range(CHUNKS):
                    w_back(slot, k).wait_recv()
            value = None
            for k in range(zn):
                deep = pl.ds(k * 2 * LANES, 2 * LANES)
                right = w_out[deep, :] if slot is None else w_next[slot, deep, :]
                term = jnp.dot(left[k], right, preferred_element_type=f32)
                value = term if value is None else value + term
            acc[rows_of(j), lane(place, cols)] = value
            then(place)

    def a_copy(i):
        return pltpu.make_async_remote_copy(
            src_ref=acc.at[rows_of(other), lane(i, cols)], dst_ref=acc_in.at[:, lane(i, cols)],
            send_sem=sem_a_s.at[i], recv_sem=sem_a_r.at[i], device_id=dev(me, other), device_id_type=MESH)

    def o_copy(i):
        return pltpu.make_async_remote_copy(
            src_ref=part.at[:, lane(i, cols)], dst_ref=out.at[:, lane(i, cols)],
            send_sem=sem_o_s.at[i], recv_sem=sem_o_r.at[i], device_id=dev(groups * core + group, side),
            device_id_type=MESH)

    for d in order:
        g_land(0, d).wait_recv()
    def give(place):
        a_copy(place).start()

    def take(place, store):
        a_copy(place).wait_recv()
        ln = lane(place, cols)
        store[:, ln] = (acc[rows_of(core), ln] + acc_in[:, ln]).astype(bf16)

    def far(place):
        pl.when(core == side)(lambda: give(place))

        @pl.when(core != side)
        def _():
            take(place, part)
            o_copy(place).start()

    def near(place):
        pl.when(core != side)(lambda: give(place))
        pl.when(core == side)(lambda: take(place, out))

    project(1 - side, True, far)
    for d in order:
        g_land(1, d).wait_recv()
    project(side, False, near)

    @pl.when(core != side)
    def _():
        for i in range(groups):
            o_copy(i).wait_recv()
            o_copy(i).wait_send()

    @pl.when(me < seq_count - 1)
    def _():
        rim_copy().wait_send()

    for d in order:
        spread(kv_own, kv_all, sem_kvh_s, sem_kvh_r, d, top).wait_send()
        spread(q_own, q_all, sem_q_s, sem_q_r, d, whole).wait_send()
        g_send(1, d).wait_send()
    for d in order[max(0, len(order) - QLAG) :]:
        spread(kv_own, kv_all, sem_kvm_s, sem_kvm_r, d, main).wait_send()
    for d in order[max(0, len(order) - GLAG) :]:
        g_send(0, d).wait_send()
    for i in range(6):
        for k in range(CHUNKS):
            w_copy(i, k).wait_send()
    for i in range(groups):
        a_copy(i).wait_send()


def fused(
    streams, short_weight, filter_modes, filter_first, filter_out, decay_rate, skip_gain, w_out
):
    f32, bf16 = jnp.float32, jnp.bfloat16
    n = lax.axis_size("seq")
    width, blk = streams.shape[1], streams.shape[2]
    cols = w_out.shape[1]
    total = n * blk
    dma = pltpu.SemaphoreType.DMA
    vmem = pltpu.VMEM
    return pl.pallas_call(
        functools.partial(mixer, n),
        out_shape=jax.ShapeDtypeStruct((blk, n * cols // 2), bf16),
        in_specs=[
            pl.BlockSpec(memory_space=pltpu.HBM) for _ in range(9)
        ],
        out_specs=pl.BlockSpec(memory_space=pltpu.VMEM),
        scratch_shapes=[
            vmem(streams.shape, bf16),
            vmem(short_weight.shape, f32),
            pltpu.SMEM(filter_modes.shape, jnp.int32),
            vmem(filter_first.shape, f32),
            vmem((filter_out.shape[0], LANES), f32),
            vmem((1, LANES), f32),
            vmem((1, LANES), f32),
            vmem(w_out.shape, bf16),
            vmem((8 * blk, 2 * blk), bf16),
            vmem((3, 8 + blk, width), f32),
            vmem((24, width), bf16),
            vmem((24, width), bf16),
            vmem((blk, width), bf16),
            vmem((blk, width), bf16),
            vmem((blk, total), bf16),
            vmem((blk, total), bf16),
            vmem((2 * blk, total), f32),
            vmem((blk, total), f32),
            vmem((blk, total), f32),
            vmem((blk, total), f32),
            vmem((2 * blk, total), bf16),
            vmem((n // 2, 2 * blk, LANES), bf16),
            vmem((n // 2, 2 * blk, 2 * LANES), bf16),
            vmem((3, *w_out.shape), bf16),
            vmem((2 * blk, n // 2 * cols), f32),
            vmem((blk, n // 2 * cols), f32),
            vmem((blk, n // 2 * cols), bf16),
            dma((11,)),
            dma((2,)),
            dma((n,)), dma((n,)),
            dma((n,)), dma((n,)),
            dma((n,)), dma((n,)),
            dma((2, n)), dma((2, n)),
            dma((6, CHUNKS)), dma((6, CHUNKS)),
            dma((n // 2,)), dma((n // 2,)),
            dma((n // 2,)), dma((n // 2,)),
        ],
        compiler_params=pltpu.CompilerParams(
            collective_id=0, has_side_effects=True, vmem_limit_bytes=56 * 1024 * 1024
        ),
    )(
        streams, short_weight, filter_modes, filter_first, filter_out,
        decay_rate.reshape(1, -1), skip_gain.reshape(1, -1), w_out, jnp.asarray(tables(blk)),
    )


def plan(
    streams, short_weight, filter_modes, filter_first, filter_out, decay_rate, skip_gain, w_out
):
    n = lax.axis_size("seq")
    width, blk = streams.shape[1], streams.shape[2]
    fits = n == 8 and lax.axis_size("chan") == 2 and lax.axis_size("grp") == 2 and blk == LANES and width == n * LANES
    fits = fits and short_weight.shape[1] <= 9 and w_out.shape[1] % LANES == 0
    form = fused if fits else local
    return form(
        streams, short_weight, filter_modes, filter_first, filter_out, decay_rate, skip_gain, w_out
    )


def solution(mesh):
    return jax.shard_map(
        plan,
        mesh=mesh,
        in_specs=(
            P(None, "chan", ("grp", "seq")),
            P(None, None, "chan"),
            P(),
            P(),
            P(None, "chan"),
            P("chan"),
            P("chan"),
            P("chan", "seq"),
        ),
        out_specs=P(("grp", "seq"), "chan"),
        check_vma=False,
    )
```

```python
import functools
import math

import jax
import jax.numpy as jnp
import numpy as np
from jax import lax
from jax.experimental import pallas as pl
from jax.experimental.pallas import tpu as pltpu
from jax.sharding import PartitionSpec as P


def shifted(value, axis, steps):
    count = lax.axis_size(axis)
    leading, last = (max(0, -steps), min(count, count - steps))
    return lax.ppermute(value, axis, [(source, source + steps) for source in range(leading, last)])


def position_filter(
    positions, mode_ints, first_layer, out_cols, decay_rates, tokens_dev, seq_count
):
    total_len = tokens_dev * seq_count
    block_idx = positions // tokens_dev
    offset_idx = positions % tokens_dev
    upper_part = mode_ints[:, None] * block_idx[None, :] % seq_count
    lower_part = mode_ints[:, None] * offset_idx[None, :] % total_len
    phase_int = (tokens_dev * upper_part + lower_part) % total_len
    phase_angle = phase_int.astype(jnp.float32) * jnp.float32(2.0 * math.pi / total_len)
    features = jnp.concatenate([jnp.cos(phase_angle), jnp.sin(phase_angle)], axis=0)
    hidden = jnp.sin(
        jnp.dot(
            first_layer.T,
            features,
            precision=lax.Precision.HIGHEST,
            preferred_element_type=jnp.float32,
        )
    )
    raw_values = jnp.dot(
        out_cols.T, hidden, precision=lax.Precision.HIGHEST, preferred_element_type=jnp.float32
    )
    time_float = positions.astype(jnp.float32)
    scaled = (
        jnp.sqrt(2.0 * decay_rates)[:, None]
        * jnp.exp(-decay_rates[:, None] * time_float[None, :])
        * raw_values
    )
    return scaled.astype(jnp.bfloat16)


def angle_table(rows_count, cols_count, modulus):
    product = (
        jnp.arange(rows_count, dtype=jnp.int32)[:, None]
        * jnp.arange(cols_count, dtype=jnp.int32)[None, :]
        % modulus
    )
    phase_angle = product.astype(jnp.float32) * jnp.float32(2.0 * math.pi / modulus)
    return (jnp.cos(phase_angle), jnp.sin(phase_angle))


def contract(form, left, right):
    return jnp.einsum(
        form, left, right, precision=lax.Precision.HIGHEST, preferred_element_type=jnp.float32
    )


def local(
    streams, short_weight, filter_modes, filter_first, filter_out, decay_rate, skip_gain, w_out
):
    seq_count = lax.axis_size("seq")
    seq_index = lax.axis_index("seq")
    width_half = streams.shape[1]
    tokens_dev = streams.shape[2]
    reach = short_weight.shape[1] - 1
    per_device = width_half // seq_count
    total_len = tokens_dev * seq_count
    rim = shifted(streams[:, :, tokens_dev - reach :], "seq", 1)
    extended = jnp.concatenate([rim, streams], axis=2).astype(jnp.float32)
    feature = short_weight[:, 0, :, None] * extended[:, :, reach:]
    for tap_index in range(1, reach + 1):
        feature = (
            feature
            + short_weight[:, tap_index, :, None]
            * extended[:, :, reach - tap_index : reach - tap_index + tokens_dev]
        )
    query = feature[0].astype(jnp.bfloat16)
    kv_product = (feature[1] * feature[2]).astype(jnp.bfloat16)
    positions = seq_index * tokens_dev + jnp.arange(tokens_dev, dtype=jnp.int32)
    filter_local = position_filter(
        positions, filter_modes, filter_first, filter_out, decay_rate, tokens_dev, seq_count
    )
    kv_channels, filter_channels = (
        lax.all_to_all(kv_product, "seq", split_axis=0, concat_axis=1, tiled=True),
        lax.all_to_all(filter_local, "seq", split_axis=0, concat_axis=1, tiled=True),
    )
    doubled = 2 * seq_count
    padded_len = 2 * total_len
    cos_outer, sin_outer = angle_table(doubled, seq_count, doubled)
    cos_twist, sin_twist = angle_table(doubled, tokens_dev, padded_len)
    cos_inner, sin_inner = angle_table(tokens_dev, tokens_dev, tokens_dev)

    def forward(signal):
        shaped = signal.astype(jnp.float32).reshape(per_device, seq_count, tokens_dev)
        a_real = contract("cpj,kp->ckj", shaped, cos_outer)
        a_imag = -contract("cpj,kp->ckj", shaped, sin_outer)
        r_real = a_real * cos_twist + a_imag * sin_twist
        r_imag = a_imag * cos_twist - a_real * sin_twist
        x_real = contract("ckj,jm->ckm", r_real, cos_inner) + contract(
            "ckj,jm->ckm", r_imag, sin_inner
        )
        x_imag = contract("ckj,jm->ckm", r_imag, cos_inner) - contract(
            "ckj,jm->ckm", r_real, sin_inner
        )
        return (x_real, x_imag)

    kv_real, kv_imag = forward(kv_channels)
    fl_real, fl_imag = forward(filter_channels)
    y_real = kv_real * fl_real - kv_imag * fl_imag
    y_imag = kv_real * fl_imag + kv_imag * fl_real
    b_real = contract("ckm,mj->ckj", y_real, cos_inner) - contract("ckm,mj->ckj", y_imag, sin_inner)
    b_imag = contract("ckm,mj->ckj", y_imag, cos_inner) + contract("ckm,mj->ckj", y_real, sin_inner)
    t_real = b_real * cos_twist - b_imag * sin_twist
    t_imag = b_real * sin_twist + b_imag * cos_twist
    conv_values = contract("ckj,kp->cpj", t_real, cos_outer) - contract(
        "ckj,kp->cpj", t_imag, sin_outer
    )
    conv_channels = (
        (conv_values * jnp.float32(1.0 / padded_len))
        .reshape(per_device, total_len)
        .astype(jnp.bfloat16)
    )
    conv_tokens = lax.all_to_all(conv_channels, "seq", split_axis=1, concat_axis=0, tiled=True)
    gated = (
        query.astype(jnp.float32)
        * (conv_tokens.astype(jnp.float32) + skip_gain[:, None] * kv_product.astype(jnp.float32))
    ).astype(jnp.bfloat16)
    partial_out = lax.dot_general(
        gated,
        lax.all_gather(w_out, "seq", axis=1, tiled=True),
        (((0,), (0,)), ((), ())),
        preferred_element_type=jnp.float32,
    )
    return lax.psum_scatter(partial_out, "chan", scatter_dimension=1, tiled=True).astype(
        jnp.bfloat16
    )


LANES = 128
CHUNKS = 4
QLAG = 7
PLAN = {'kv': ('x0', 'x1', 'x2', 'x3'), 'top': (), 'q': ((), (), (), (), (), (), ('z0', 'z1', 'z2', 'z3', 'X0', 'X1', 'X2', 'X3')), 'land': ('Z0',), 'conv': ('Z1', 'Z2'), 'gate': ((), (), (), ('Z3', 'D0'), (), ('D1',), (), ()), 'g0': ('D2',), 'g1': ((), (), (), ('D3',), (), (), ()), 'far': ((), (), (), ())}
MESH = pl.DeviceIdType.MESH


def tables(block):
    size = 2 * block
    steps = np.arange(size)
    angle = 2.0 * np.pi * (np.outer(np.arange(block), steps) % size) / size
    forward = np.concatenate([np.cos(angle), -np.sin(angle)], axis=0)
    forward[block] = np.cos(np.pi * steps)
    weight = np.full((size, 1), 2.0 / size)
    weight[0] = weight[block] = 1.0 / size
    inverse = (forward * weight).T[block:]
    upper = np.asarray(forward, dtype=jnp.bfloat16)
    lower = np.asarray(forward - upper.astype(np.float64), dtype=jnp.bfloat16)
    both = np.concatenate([upper[:, :block], lower[:, :block]], axis=1)
    unit = np.eye(block, size)
    return np.concatenate(
        [upper, lower, both, np.asarray(inverse, jnp.bfloat16), np.asarray(unit, jnp.bfloat16)], axis=0
    )


def split_pi():
    parts, rest = [], math.pi
    for bits in (10, 22):
        part = math.floor(rest * 2.0**bits) / 2.0**bits
        parts.append(part)
        rest -= part
    return (*parts, rest)


def sine(value):
    f32 = jnp.float32
    count = jnp.floor(value * f32(1.0 / math.pi) + f32(0.5))
    rest = value
    for part in split_pi():
        rest = rest - count * f32(part)
    half = count * f32(0.5)
    sign = f32(1.0) - f32(4.0) * (half - jnp.floor(half))
    square = rest * rest
    series = f32(0.0)
    for degree in range(13, 1, -2):
        series = (series + f32((-1.0) ** (degree // 2) / math.factorial(degree))) * square
    return sign * (rest + rest * series)


def mixer(
    seq_count, streams_h, short_h, modes_h, first_h, filter_h, decay_h, skip_h, w_h, table_h, out,
    streams, short_weight, modes, first, filter_cols, decay, skip, w_out, table,
    xt, rim_out, rim_in, kv_own, q_own, kv_all, q_all, spec_x, spec_r, spec_i, spec_n, spec_y,
    gate_own, gate_all, w_next, acc, acc_in, part,
    sem_in, sem_rim, sem_kvm_s, sem_kvm_r, sem_kvh_s, sem_kvh_r, sem_q_s, sem_q_r, sem_g_s, sem_g_r,
    sem_w_s, sem_w_r, sem_a_s, sem_a_r, sem_o_s, sem_o_r,
):
    f32, bf16 = jnp.float32, jnp.bfloat16
    blk = streams.shape[2]
    size = 2 * blk
    taps = short_weight.shape[1]
    total = seq_count * blk
    cols = w_out.shape[1]
    zn = seq_count // 2
    groups = seq_count // 2
    grp = lax.axis_index("grp")
    me = lax.axis_index("seq")
    core = lax.axis_index("chan")
    other = 1 - core
    z = me // 2
    x = me % 2
    side = me // groups
    group = me % groups

    def dev(seq, chan):
        return (grp, seq, chan)

    def lane(i, n=LANES):
        return pl.ds(pl.multiple_of(i * n, n), n)

    barrier = pltpu.get_barrier_semaphore()
    for d in range(1, seq_count):
        for ch in (core, other):
            pl.semaphore_signal(barrier, inc=1, device_id=dev((me + d) % seq_count, ch), device_id_type=MESH)
    for near in (dev(me, other), (1 - grp, me, core)):
        pl.semaphore_signal(barrier, inc=1, device_id=near, device_id_type=MESH)

    here = lane(me)
    loads = (
        (table_h, table),
        (streams_h.at[0], streams.at[0]),
        (streams_h.at[1], streams.at[1]),
        (streams_h.at[2], streams.at[2]),
        (short_h, short_weight),
        (modes_h, modes),
        (first_h, first),
        (filter_h.at[:, here], filter_cols),
        (decay_h.at[:, here], decay),
        (skip_h.at[:, here], skip),
        (w_h, w_out),
    )

    def load(i):
        return pltpu.make_async_copy(loads[i][0], loads[i][1], sem_in.at[i])

    for i in range(len(loads)):
        load(i).start()
    load(0).wait()
    eye = table[4 * blk + 2 * blk + blk : 4 * blk + 2 * blk + 2 * blk, :blk]
    for st in range(3):
        load(1 + st).wait()
        turned = lax.dot_general(eye, streams[st], (((1,), (1,)), ((), ())), preferred_element_type=f32)
        xt[st, 8:, :] = turned
    rim_out[...] = jnp.concatenate([xt[st, blk:, :] for st in range(3)], axis=0).astype(bf16)

    def features(rows):
        def body(l, carry):
            ln = lane(l)
            for r0 in rows:
                feat = []
                for st in range(3):
                    total_f = short_weight[st, pl.ds(0, 1), ln] * xt[st, pl.ds(8 + r0, 16), ln]
                    for i in range(1, taps):
                        total_f = total_f + short_weight[st, pl.ds(i, 1), ln] * xt[st, pl.ds(8 + r0 - i, 16), ln]
                    feat.append(total_f)
                q_own[pl.ds(r0, 16), ln] = feat[0].astype(bf16)
                kv_own[pl.ds(r0, 16), ln] = (feat[1] * feat[2]).astype(bf16)
            return carry

        lax.fori_loop(0, seq_count, body, 0)

    load(4).wait()
    features(range(16, blk, 16))

    pl.semaphore_wait(barrier, 2 * seq_count)

    def rim_copy():
        return pltpu.make_async_remote_copy(
            src_ref=rim_out, dst_ref=rim_in, send_sem=sem_rim.at[0], recv_sem=sem_rim.at[1],
            device_id=dev((me + 1) % seq_count, core), device_id_type=MESH)

    def spread(own, every, send, recv, d, rows):
        to = (me + d) % seq_count
        return pltpu.make_async_remote_copy(
            src_ref=own.at[rows, lane(to)], dst_ref=every.at[rows, lane(me)],
            send_sem=send.at[d], recv_sem=recv.at[d], device_id=dev(to, core), device_id_type=MESH)

    def landing(own, every, send, recv, d, rows):
        source = (me + seq_count - d) % seq_count
        return pltpu.make_async_remote_copy(
            src_ref=own.at[rows, lane(source)], dst_ref=every.at[rows, lane(source)],
            send_sem=send.at[d], recv_sem=recv.at[d], device_id=dev(source, core), device_id_type=MESH)

    main, top, whole = pl.ds(16, blk - 16), pl.ds(0, 16), pl.ds(0, blk)
    order = (4, 3, 5, 2, 6, 1, 7) if seq_count == 8 else tuple(range(1, seq_count))

    @pl.when(me < seq_count - 1)
    def _():
        rim_copy().start()

    for d in order:
        spread(kv_own, kv_all, sem_kvm_s, sem_kvm_r, d, main).start()

    part_rows = w_out.shape[0] // 2
    step_rows = part_rows // CHUNKS
    beside = dev(me + 1 - 2 * x, core)
    above = dev(me + 2 - 4 * (z % 2), core)
    across = (1 - grp, me, core)
    w_source = (w_h, w_h, w_next.at[1], w_next.at[0], w_next.at[1], w_next.at[2])
    w_slot = (0, 1, 2, 0, 1, 2)
    w_to = (beside, above, beside, across, across, across)

    def chunk(side_y, k):
        return pl.ds(pl.multiple_of(side_y * part_rows + k * step_rows, step_rows), step_rows)

    def w_copy(i, k):
        return pltpu.make_async_remote_copy(
            src_ref=w_source[i].at[chunk(grp, k), :], dst_ref=w_next.at[w_slot[i], chunk(grp, k), :],
            send_sem=sem_w_s.at[i, k], recv_sem=sem_w_r.at[i, k], device_id=w_to[i], device_id_type=MESH)

    def w_back(slot, k):
        return pltpu.make_async_remote_copy(
            src_ref=w_next.at[slot, chunk(1 - grp, k), :], dst_ref=w_next.at[slot, chunk(1 - grp, k), :],
            send_sem=sem_w_s.at[3 + slot, k], recv_sem=sem_w_r.at[3 + slot, k], device_id=across, device_id_type=MESH)

    def forward(i, k):
        w_copy(i, k).wait_recv()
        for nxt in ((3,), (4, 2), (5,))[i]:
            w_copy(nxt, k).start()

    def w_steps(*names):
        for name in names:
            i, k = "xzdXZD".index(name[0]), int(name[1:])
            if i < 3:
                w_copy(i, k).start()
            else:
                forward(i - 3, k)

    w_steps(*PLAN["kv"])

    load(5).wait()
    bands = modes.shape[0]
    band = lax.broadcasted_iota(jnp.int32, (bands, LANES), 0)
    mode = jnp.zeros((bands, LANES), jnp.int32)
    for b in range(bands):
        mode = jnp.where(band == b, modes[b], mode)
    mode = jnp.concatenate([mode] * (total // LANES), axis=1)
    steps = lax.broadcasted_iota(jnp.int32, (bands, total), 1)
    phase = (mode * steps) & (total - 1)
    turn_unit = f32(2.0 * math.pi / total)
    positional = sine(jnp.concatenate([phase + total // 4, phase], axis=0).astype(f32) * turn_unit)
    load(6).wait()
    hidden = sine(lax.dot_general(
        first[...], positional, (((0,), (0,)), ((), ())), precision=lax.Precision.HIGHEST,
        preferred_element_type=f32))
    load(7).wait()
    raw = lax.dot_general(
        hidden, filter_cols[...], (((0,), (0,)), ((), ())), precision=lax.Precision.HIGHEST,
        preferred_element_type=f32)
    load(8).wait()
    rate = decay[...]
    root = jnp.sqrt(2.0 * rate)
    pieces = []
    for r in range(seq_count):
        time = (lax.broadcasted_iota(jnp.int32, (blk, LANES), 0) + r * blk).astype(f32)
        pieces.append((root * jnp.exp(-rate * time) * raw[r * blk : (r + 1) * blk]).astype(bf16))
    now = jnp.concatenate(pieces, axis=1)
    before = jnp.concatenate([jnp.zeros((blk, LANES), bf16)] + pieces[:-1], axis=1)
    window = jnp.concatenate([before, now], axis=0)
    spectrum = jnp.dot(table[:size, :], window, preferred_element_type=f32) + jnp.dot(
        table[size : 2 * size, :], window, preferred_element_type=f32)
    row0 = lax.broadcasted_iota(jnp.int32, (blk, total), 0) == 0
    real, imag = spectrum[:blk], spectrum[blk:]
    spec_r[...] = real
    spec_i[...] = jnp.where(row0, 0.0, imag)
    spec_n[...] = jnp.where(row0, imag, real)

    @pl.when(me > 0)
    def _():
        rim_copy().wait_recv()
        for st in range(3):
            xt[st, 0:8, :] = rim_in[8 * st : 8 * st + 8, :].astype(f32)

    @pl.when(me == 0)
    def _():
        for st in range(3):
            xt[st, 0:8, :] = jnp.zeros((8, xt.shape[2]), f32)

    features((0,))
    for d in order:
        spread(kv_own, kv_all, sem_kvh_s, sem_kvh_r, d, top).start()
    w_steps(*PLAN["top"])
    for i, d in enumerate(order):
        if i >= QLAG:
            spread(kv_own, kv_all, sem_kvm_s, sem_kvm_r, order[i - QLAG], main).wait_send()
        spread(q_own, q_all, sem_q_s, sem_q_r, d, whole).start()
        w_steps(*PLAN["q"][i])
    kv_all[:, lane(me)] = kv_own[:, lane(me)]
    q_all[:, lane(me)] = q_own[:, lane(me)]

    for d in order:
        landing(kv_own, kv_all, sem_kvm_s, sem_kvm_r, d, main).wait_recv()
    for d in order:
        landing(kv_own, kv_all, sem_kvh_s, sem_kvh_r, d, top).wait_recv()
    w_steps(*PLAN["land"])
    kv = kv_all[...]
    spec_x[...] = jnp.dot(
        table[2 * size : 3 * size, :], jnp.concatenate([kv, kv], axis=0), preferred_element_type=f32)

    def product(i, carry):
        lo = pl.ds(pl.multiple_of(i * 16, 16), 16)
        hi = pl.ds(pl.multiple_of(blk + i * 16, 16), 16)
        for p in range(seq_count):
            y_real = y_imag = None
            for s in range(p + 1):
                sl, fl = pl.ds(s * LANES, LANES), pl.ds((p - s) * LANES, LANES)
                xr, xi = spec_x[lo, sl], spec_x[hi, sl]
                hr, him, hn = spec_r[lo, fl], spec_i[lo, fl], spec_n[lo, fl]
                tr = xr * hr - xi * him
                ti = xr * him + xi * hn
                y_real = tr if y_real is None else y_real + tr
                y_imag = ti if y_imag is None else y_imag + ti
            spec_y[lo, pl.ds(p * LANES, LANES)] = y_real.astype(bf16)
            spec_y[hi, pl.ds(p * LANES, LANES)] = y_imag.astype(bf16)
        return carry

    lax.fori_loop(0, blk // 16, product, 0)
    spec_r[...] = jnp.dot(table[3 * size : 3 * size + blk, :], spec_y[...], preferred_element_type=f32)
    w_steps(*PLAN["conv"])
    def rows_of(j):
        return pl.ds(pl.multiple_of(j * blk, blk), blk)

    def g_send(turn, d):
        to = (me + d) % seq_count
        far = to // groups
        rows = rows_of(1 - far if turn == 0 else far)
        return pltpu.make_async_remote_copy(
            src_ref=gate_own.at[to % groups, rows, :], dst_ref=gate_all.at[z, rows, lane(x)],
            send_sem=sem_g_s.at[turn, d], recv_sem=sem_g_r.at[turn, d], device_id=dev(to, core), device_id_type=MESH)

    def g_land(turn, d):
        source = (me + seq_count - d) % seq_count
        rows = rows_of(1 - side if turn == 0 else side)
        return pltpu.make_async_remote_copy(
            src_ref=gate_own.at[0, rows, :], dst_ref=gate_all.at[source // 2, rows, lane(source % 2)],
            send_sem=sem_g_s.at[turn, d], recv_sem=sem_g_r.at[turn, d], device_id=dev(source, core),
            device_id_type=MESH)

    load(9).wait()
    gain = skip[...]
    for i, d in enumerate((0, *order)):
        w_steps(*PLAN["gate"][i])
        if d:
            landing(q_own, q_all, sem_q_s, sem_q_r, d, whole).wait_recv()
        p = (me + seq_count - d) % seq_count
        sl = lane(p)
        inner = spec_r[:, sl].astype(bf16).astype(f32) + gain * kv_all[:, sl].astype(f32)
        gate_own[p % groups, rows_of(p // groups), :] = (q_all[:, sl].astype(f32) * inner).astype(bf16)
        if d != groups:
            g_send(0, (groups - d) % seq_count).start()
    w_steps(*PLAN["g0"])
    for i, d in enumerate(order):
        g_send(1, seq_count - d).start()
        w_steps(*PLAN["g1"][i])
    gate_all[z, :, lane(x)] = gate_own[group]
    load(10).wait()

    flip_x, flip_z = 1 - 2 * x, 2 - 4 * (z % 2)
    places = (group, group + flip_z, group + flip_x, group + flip_x + flip_z)
    slots = (None, 1, 0, 2)

    def project(j, first_turn, then):
        left = [gate_all[k, rows_of(j), :] for k in range(zn)]
        for i, (place, slot) in enumerate(zip(places, slots)):
            if first_turn:
                w_steps(*PLAN["far"][i])
            if slot is not None and first_turn:
                for k in range(CHUNKS):
                    w_back(slot, k).wait_recv()
            value = None
            for k in range(zn):
                deep = pl.ds(k * 2 * LANES, 2 * LANES)
                right = w_out[deep, :] if slot is None else w_next[slot, deep, :]
                term = jnp.dot(left[k], right, preferred_element_type=f32)
                value = term if value is None else value + term
            acc[rows_of(j), lane(place, cols)] = value
            then(place)

    def a_copy(i):
        return pltpu.make_async_remote_copy(
            src_ref=acc.at[rows_of(other), lane(i, cols)], dst_ref=acc_in.at[:, lane(i, cols)],
            send_sem=sem_a_s.at[i], recv_sem=sem_a_r.at[i], device_id=dev(me, other), device_id_type=MESH)

    def o_copy(i):
        return pltpu.make_async_remote_copy(
            src_ref=part.at[:, lane(i, cols)], dst_ref=out.at[:, lane(i, cols)],
            send_sem=sem_o_s.at[i], recv_sem=sem_o_r.at[i], device_id=dev(groups * core + group, side),
            device_id_type=MESH)

    for d in order:
        g_land(0, d).wait_recv()
    def give(place):
        a_copy(place).start()

    def take(place, store):
        a_copy(place).wait_recv()
        ln = lane(place, cols)
        store[:, ln] = (acc[rows_of(core), ln] + acc_in[:, ln]).astype(bf16)

    def far(place):
        pl.when(core == side)(lambda: give(place))

        @pl.when(core != side)
        def _():
            take(place, part)
            o_copy(place).start()

    def near(place):
        pl.when(core != side)(lambda: give(place))
        pl.when(core == side)(lambda: take(place, out))

    project(1 - side, True, far)
    for d in order:
        g_land(1, d).wait_recv()
    project(side, False, near)

    @pl.when(core != side)
    def _():
        for i in range(groups):
            o_copy(i).wait_recv()
            o_copy(i).wait_send()

    @pl.when(me < seq_count - 1)
    def _():
        rim_copy().wait_send()

    for d in order:
        spread(kv_own, kv_all, sem_kvh_s, sem_kvh_r, d, top).wait_send()
        spread(q_own, q_all, sem_q_s, sem_q_r, d, whole).wait_send()
        g_send(0, d).wait_send()
        g_send(1, d).wait_send()
    for d in order[max(0, len(order) - QLAG) :]:
        spread(kv_own, kv_all, sem_kvm_s, sem_kvm_r, d, main).wait_send()
    for i in range(6):
        for k in range(CHUNKS):
            w_copy(i, k).wait_send()
    for i in range(groups):
        a_copy(i).wait_send()


def fused(
    streams, short_weight, filter_modes, filter_first, filter_out, decay_rate, skip_gain, w_out
):
    f32, bf16 = jnp.float32, jnp.bfloat16
    n = lax.axis_size("seq")
    width, blk = streams.shape[1], streams.shape[2]
    cols = w_out.shape[1]
    total = n * blk
    dma = pltpu.SemaphoreType.DMA
    vmem = pltpu.VMEM
    return pl.pallas_call(
        functools.partial(mixer, n),
        out_shape=pltpu.VMEM((blk, n * cols // 2), bf16),
        in_specs=[
            pl.BlockSpec(memory_space=pltpu.HBM) for _ in range(9)
        ],
        out_specs=pl.BlockSpec(memory_space=pltpu.VMEM),
        scratch_shapes=[
            vmem(streams.shape, bf16),
            vmem(short_weight.shape, f32),
            pltpu.SMEM(filter_modes.shape, jnp.int32),
            vmem(filter_first.shape, f32),
            vmem((filter_out.shape[0], LANES), f32),
            vmem((1, LANES), f32),
            vmem((1, LANES), f32),
            vmem(w_out.shape, bf16),
            vmem((8 * blk, 2 * blk), bf16),
            vmem((3, 8 + blk, width), f32),
            vmem((24, width), bf16),
            vmem((24, width), bf16),
            vmem((blk, width), bf16),
            vmem((blk, width), bf16),
            vmem((blk, total), bf16),
            vmem((blk, total), bf16),
            vmem((2 * blk, total), f32),
            vmem((blk, total), f32),
            vmem((blk, total), f32),
            vmem((blk, total), f32),
            vmem((2 * blk, total), bf16),
            vmem((n // 2, 2 * blk, LANES), bf16),
            vmem((n // 2, 2 * blk, 2 * LANES), bf16),
            vmem((3, *w_out.shape), bf16),
            vmem((2 * blk, n // 2 * cols), f32),
            vmem((blk, n // 2 * cols), f32),
            vmem((blk, n // 2 * cols), bf16),
            dma((11,)),
            dma((2,)),
            dma((n,)), dma((n,)),
            dma((n,)), dma((n,)),
            dma((n,)), dma((n,)),
            dma((2, n)), dma((2, n)),
            dma((6, CHUNKS)), dma((6, CHUNKS)),
            dma((n // 2,)), dma((n // 2,)),
            dma((n // 2,)), dma((n // 2,)),
        ],
        compiler_params=pltpu.CompilerParams(
            collective_id=0, has_side_effects=True, vmem_limit_bytes=56 * 1024 * 1024
        ),
    )(
        streams, short_weight, filter_modes, filter_first, filter_out,
        decay_rate.reshape(1, -1), skip_gain.reshape(1, -1), w_out, jnp.asarray(tables(blk)),
    )


def plan(
    streams, short_weight, filter_modes, filter_first, filter_out, decay_rate, skip_gain, w_out
):
    n = lax.axis_size("seq")
    width, blk = streams.shape[1], streams.shape[2]
    fits = n == 8 and lax.axis_size("chan") == 2 and lax.axis_size("grp") == 2 and blk == LANES and width == n * LANES
    fits = fits and short_weight.shape[1] <= 9 and w_out.shape[1] % LANES == 0
    form = fused if fits else local
    return form(
        streams, short_weight, filter_modes, filter_first, filter_out, decay_rate, skip_gain, w_out
    )


def solution(mesh):
    return jax.shard_map(
        plan,
        mesh=mesh,
        in_specs=(
            P(None, "chan", ("grp", "seq")),
            P(None, None, "chan"),
            P(),
            P(),
            P(None, "chan"),
            P("chan"),
            P("chan"),
            P("chan", "seq"),
        ),
        out_specs=P(("grp", "seq"), "chan"),
        check_vma=False,
    )
```

```python
import functools
import math

import jax
import jax.numpy as jnp
import numpy as np
from jax import lax
from jax.experimental import pallas as pl
from jax.experimental.pallas import tpu as pltpu
from jax.sharding import PartitionSpec as P


def shifted(value, axis, steps):
    count = lax.axis_size(axis)
    leading, last = (max(0, -steps), min(count, count - steps))
    return lax.ppermute(value, axis, [(source, source + steps) for source in range(leading, last)])


def position_filter(
    positions, mode_ints, first_layer, out_cols, decay_rates, tokens_dev, seq_count
):
    total_len = tokens_dev * seq_count
    block_idx = positions // tokens_dev
    offset_idx = positions % tokens_dev
    upper_part = mode_ints[:, None] * block_idx[None, :] % seq_count
    lower_part = mode_ints[:, None] * offset_idx[None, :] % total_len
    phase_int = (tokens_dev * upper_part + lower_part) % total_len
    phase_angle = phase_int.astype(jnp.float32) * jnp.float32(2.0 * math.pi / total_len)
    features = jnp.concatenate([jnp.cos(phase_angle), jnp.sin(phase_angle)], axis=0)
    hidden = jnp.sin(
        jnp.dot(
            first_layer.T,
            features,
            precision=lax.Precision.HIGHEST,
            preferred_element_type=jnp.float32,
        )
    )
    raw_values = jnp.dot(
        out_cols.T, hidden, precision=lax.Precision.HIGHEST, preferred_element_type=jnp.float32
    )
    time_float = positions.astype(jnp.float32)
    scaled = (
        jnp.sqrt(2.0 * decay_rates)[:, None]
        * jnp.exp(-decay_rates[:, None] * time_float[None, :])
        * raw_values
    )
    return scaled.astype(jnp.bfloat16)


def angle_table(rows_count, cols_count, modulus):
    product = (
        jnp.arange(rows_count, dtype=jnp.int32)[:, None]
        * jnp.arange(cols_count, dtype=jnp.int32)[None, :]
        % modulus
    )
    phase_angle = product.astype(jnp.float32) * jnp.float32(2.0 * math.pi / modulus)
    return (jnp.cos(phase_angle), jnp.sin(phase_angle))


def contract(form, left, right):
    return jnp.einsum(
        form, left, right, precision=lax.Precision.HIGHEST, preferred_element_type=jnp.float32
    )


def local(
    streams, short_weight, filter_modes, filter_first, filter_out, decay_rate, skip_gain, w_out
):
    seq_count = lax.axis_size("seq")
    seq_index = lax.axis_index("seq")
    width_half = streams.shape[1]
    tokens_dev = streams.shape[2]
    reach = short_weight.shape[1] - 1
    per_device = width_half // seq_count
    total_len = tokens_dev * seq_count
    rim = shifted(streams[:, :, tokens_dev - reach :], "seq", 1)
    extended = jnp.concatenate([rim, streams], axis=2).astype(jnp.float32)
    feature = short_weight[:, 0, :, None] * extended[:, :, reach:]
    for tap_index in range(1, reach + 1):
        feature = (
            feature
            + short_weight[:, tap_index, :, None]
            * extended[:, :, reach - tap_index : reach - tap_index + tokens_dev]
        )
    query = feature[0].astype(jnp.bfloat16)
    kv_product = (feature[1] * feature[2]).astype(jnp.bfloat16)
    positions = seq_index * tokens_dev + jnp.arange(tokens_dev, dtype=jnp.int32)
    filter_local = position_filter(
        positions, filter_modes, filter_first, filter_out, decay_rate, tokens_dev, seq_count
    )
    kv_channels, filter_channels = (
        lax.all_to_all(kv_product, "seq", split_axis=0, concat_axis=1, tiled=True),
        lax.all_to_all(filter_local, "seq", split_axis=0, concat_axis=1, tiled=True),
    )
    doubled = 2 * seq_count
    padded_len = 2 * total_len
    cos_outer, sin_outer = angle_table(doubled, seq_count, doubled)
    cos_twist, sin_twist = angle_table(doubled, tokens_dev, padded_len)
    cos_inner, sin_inner = angle_table(tokens_dev, tokens_dev, tokens_dev)

    def forward(signal):
        shaped = signal.astype(jnp.float32).reshape(per_device, seq_count, tokens_dev)
        a_real = contract("cpj,kp->ckj", shaped, cos_outer)
        a_imag = -contract("cpj,kp->ckj", shaped, sin_outer)
        r_real = a_real * cos_twist + a_imag * sin_twist
        r_imag = a_imag * cos_twist - a_real * sin_twist
        x_real = contract("ckj,jm->ckm", r_real, cos_inner) + contract(
            "ckj,jm->ckm", r_imag, sin_inner
        )
        x_imag = contract("ckj,jm->ckm", r_imag, cos_inner) - contract(
            "ckj,jm->ckm", r_real, sin_inner
        )
        return (x_real, x_imag)

    kv_real, kv_imag = forward(kv_channels)
    fl_real, fl_imag = forward(filter_channels)
    y_real = kv_real * fl_real - kv_imag * fl_imag
    y_imag = kv_real * fl_imag + kv_imag * fl_real
    b_real = contract("ckm,mj->ckj", y_real, cos_inner) - contract("ckm,mj->ckj", y_imag, sin_inner)
    b_imag = contract("ckm,mj->ckj", y_imag, cos_inner) + contract("ckm,mj->ckj", y_real, sin_inner)
    t_real = b_real * cos_twist - b_imag * sin_twist
    t_imag = b_real * sin_twist + b_imag * cos_twist
    conv_values = contract("ckj,kp->cpj", t_real, cos_outer) - contract(
        "ckj,kp->cpj", t_imag, sin_outer
    )
    conv_channels = (
        (conv_values * jnp.float32(1.0 / padded_len))
        .reshape(per_device, total_len)
        .astype(jnp.bfloat16)
    )
    conv_tokens = lax.all_to_all(conv_channels, "seq", split_axis=1, concat_axis=0, tiled=True)
    gated = (
        query.astype(jnp.float32)
        * (conv_tokens.astype(jnp.float32) + skip_gain[:, None] * kv_product.astype(jnp.float32))
    ).astype(jnp.bfloat16)
    partial_out = lax.dot_general(
        gated,
        lax.all_gather(w_out, "seq", axis=1, tiled=True),
        (((0,), (0,)), ((), ())),
        preferred_element_type=jnp.float32,
    )
    return lax.psum_scatter(partial_out, "chan", scatter_dimension=1, tiled=True).astype(
        jnp.bfloat16
    )


LANES = 128
CHUNKS = 4
QLAG = 7
LATE = False
PLAN = {'near': ('z0', 'x0', 'z1', 'x1'), 'kv': ('x2', 'x3'), 'top': (), 'q': ((), (), (), (), (), (), ('z2', 'z3', 'X0', 'X1', 'Z0', 'Z1', 'X2')), 'land': (), 'conv': ('X3', 'Z2'), 'gate': ((), (), (), ('Z3', 'D0'), (), (), (), ()), 'g0': ('D1', 'D2'), 'g1': ((), (), (), ('D3',), (), (), ()), 'far': ((), (), (), ())}
MESH = pl.DeviceIdType.MESH


def tables(block):
    size = 2 * block
    steps = np.arange(size)
    angle = 2.0 * np.pi * (np.outer(np.arange(block), steps) % size) / size
    forward = np.concatenate([np.cos(angle), -np.sin(angle)], axis=0)
    forward[block] = np.cos(np.pi * steps)
    weight = np.full((size, 1), 2.0 / size)
    weight[0] = weight[block] = 1.0 / size
    inverse = (forward * weight).T[block:]
    upper = np.asarray(forward, dtype=jnp.bfloat16)
    lower = np.asarray(forward - upper.astype(np.float64), dtype=jnp.bfloat16)
    both = np.concatenate([upper[:, :block], lower[:, :block]], axis=1)
    unit = np.eye(block, size)
    return np.concatenate(
        [upper, lower, both, np.asarray(inverse, jnp.bfloat16), np.asarray(unit, jnp.bfloat16)], axis=0
    )


def split_pi():
    parts, rest = [], math.pi
    for bits in (10, 22):
        part = math.floor(rest * 2.0**bits) / 2.0**bits
        parts.append(part)
        rest -= part
    return (*parts, rest)


def sine(value):
    f32 = jnp.float32
    count = jnp.floor(value * f32(1.0 / math.pi) + f32(0.5))
    rest = value
    for part in split_pi():
        rest = rest - count * f32(part)
    half = count * f32(0.5)
    sign = f32(1.0) - f32(4.0) * (half - jnp.floor(half))
    square = rest * rest
    series = f32(0.0)
    for degree in range(13, 1, -2):
        series = (series + f32((-1.0) ** (degree // 2) / math.factorial(degree))) * square
    return sign * (rest + rest * series)


def mixer(
    seq_count, streams_h, short_h, modes_h, first_h, filter_h, decay_h, skip_h, w_h, table_h, out,
    streams, short_weight, modes, first, filter_cols, decay, skip, w_out, table,
    xt, rim_out, rim_in, kv_own, q_own, kv_all, q_all, spec_x, spec_r, spec_i, spec_n, spec_y,
    gate_own, gate_all, w_next, acc, acc_in, part,
    sem_far, sem_in, sem_rim, sem_kvm_s, sem_kvm_r, sem_kvh_s, sem_kvh_r, sem_q_s, sem_q_r, sem_g_s, sem_g_r,
    sem_w_s, sem_w_r, sem_a_s, sem_a_r, sem_o_s, sem_o_r,
):
    f32, bf16 = jnp.float32, jnp.bfloat16
    blk = streams.shape[2]
    size = 2 * blk
    taps = short_weight.shape[1]
    total = seq_count * blk
    cols = w_out.shape[1]
    zn = seq_count // 2
    groups = seq_count // 2
    grp = lax.axis_index("grp")
    me = lax.axis_index("seq")
    core = lax.axis_index("chan")
    other = 1 - core
    z = me // 2
    x = me % 2
    side = me // groups
    group = me % groups

    def dev(seq, chan):
        return (grp, seq, chan)

    def lane(i, n=LANES):
        return pl.ds(pl.multiple_of(i * n, n), n)

    barrier = pltpu.get_barrier_semaphore()
    def within(dz):
        return jnp.logical_and(z + dz >= 0, z + dz < zn)

    def hello(to):
        pl.semaphore_signal(barrier, inc=1, device_id=to, device_id_type=MESH)

    for dz in (1, -1):

        @pl.when(within(dz))
        def _():
            for px in range(2):
                for ch in (core, other):
                    hello(dev((z + dz) * 2 + px, ch))

    for near in (dev(z * 2 + 1 - x, core), dev(z * 2 + 1 - x, other), dev(me, other), (1 - grp, me, core)):
        hello(near)

    def tell(level):
        for i, dz in enumerate((1, -1)):

            @pl.when(jnp.logical_and(within(-dz), within(dz * level)))
            def _():
                pl.semaphore_signal(
                    sem_far.at[level - 1, i], inc=1, device_id=dev(me - 2 * dz, core), device_id_type=MESH)

    def hear(level):
        for i, dz in enumerate((1, -1)):

            @pl.when(within(dz * (level + 1)))
            def _():
                pl.semaphore_wait(sem_far.at[level - 1, i], 1)

    here = lane(me)
    loads = (
        (table_h, table),
        (streams_h.at[0], streams.at[0]),
        (streams_h.at[1], streams.at[1]),
        (streams_h.at[2], streams.at[2]),
        (short_h, short_weight),
        (modes_h, modes),
        (first_h, first),
        (filter_h.at[:, here], filter_cols),
        (decay_h.at[:, here], decay),
        (skip_h.at[:, here], skip),
        (w_h, w_out),
    )

    def load(i):
        return pltpu.make_async_copy(loads[i][0], loads[i][1], sem_in.at[i])

    for i in range(len(loads)):
        load(i).start()
    load(0).wait()
    eye = table[4 * blk + 2 * blk + blk : 4 * blk + 2 * blk + 2 * blk, :blk]
    for st in range(3):
        load(1 + st).wait()
        turned = lax.dot_general(eye, streams[st], (((1,), (1,)), ((), ())), preferred_element_type=f32)
        xt[st, 8:, :] = turned
    rim_out[...] = jnp.concatenate([xt[st, blk:, :] for st in range(3)], axis=0).astype(bf16)

    def features(rows):
        def body(l, carry):
            ln = lane(l)
            for r0 in rows:
                feat = []
                for st in range(3):
                    total_f = short_weight[st, pl.ds(0, 1), ln] * xt[st, pl.ds(8 + r0, 16), ln]
                    for i in range(1, taps):
                        total_f = total_f + short_weight[st, pl.ds(i, 1), ln] * xt[st, pl.ds(8 + r0 - i, 16), ln]
                    feat.append(total_f)
                q_own[pl.ds(r0, 16), ln] = feat[0].astype(bf16)
                kv_own[pl.ds(r0, 16), ln] = (feat[1] * feat[2]).astype(bf16)
            return carry

        lax.fori_loop(0, seq_count, body, 0)

    load(4).wait()
    if LATE:
        features(range(16, blk, 16))
    inner = jnp.logical_and(within(1), within(-1))
    pl.when(inner)(lambda: pl.semaphore_wait(barrier, 12))
    pl.when(jnp.logical_not(inner))(lambda: pl.semaphore_wait(barrier, 8))
    tell(1)

    def rim_copy():
        return pltpu.make_async_remote_copy(
            src_ref=rim_out, dst_ref=rim_in, send_sem=sem_rim.at[0], recv_sem=sem_rim.at[1],
            device_id=dev((me + 1) % seq_count, core), device_id_type=MESH)

    def spread(own, every, send, recv, d, rows):
        to = (me + d) % seq_count
        return pltpu.make_async_remote_copy(
            src_ref=own.at[rows, lane(to)], dst_ref=every.at[rows, lane(me)],
            send_sem=send.at[d], recv_sem=recv.at[d], device_id=dev(to, core), device_id_type=MESH)

    def landing(own, every, send, recv, d, rows):
        source = (me + seq_count - d) % seq_count
        return pltpu.make_async_remote_copy(
            src_ref=own.at[rows, lane(source)], dst_ref=every.at[rows, lane(source)],
            send_sem=send.at[d], recv_sem=recv.at[d], device_id=dev(source, core), device_id_type=MESH)

    main, top, whole = pl.ds(16, blk - 16), pl.ds(0, 16), pl.ds(0, blk)
    order = (4, 3, 5, 2, 6, 1, 7) if seq_count == 8 else tuple(range(1, seq_count))

    part_rows = w_out.shape[0] // 2
    step_rows = part_rows // CHUNKS
    beside = dev(me + 1 - 2 * x, core)
    above = dev(me + 2 - 4 * (z % 2), core)
    across = (1 - grp, me, core)
    w_source = (w_h, w_h, w_next.at[1], w_next.at[0], w_next.at[1], w_next.at[2])
    w_slot = (0, 1, 2, 0, 1, 2)
    w_to = (beside, above, beside, across, across, across)

    def chunk(side_y, k):
        return pl.ds(pl.multiple_of(side_y * part_rows + k * step_rows, step_rows), step_rows)

    def w_copy(i, k):
        return pltpu.make_async_remote_copy(
            src_ref=w_source[i].at[chunk(grp, k), :], dst_ref=w_next.at[w_slot[i], chunk(grp, k), :],
            send_sem=sem_w_s.at[i, k], recv_sem=sem_w_r.at[i, k], device_id=w_to[i], device_id_type=MESH)

    def w_back(slot, k):
        return pltpu.make_async_remote_copy(
            src_ref=w_next.at[slot, chunk(1 - grp, k), :], dst_ref=w_next.at[slot, chunk(1 - grp, k), :],
            send_sem=sem_w_s.at[3 + slot, k], recv_sem=sem_w_r.at[3 + slot, k], device_id=across, device_id_type=MESH)

    def forward(i, k):
        w_copy(i, k).wait_recv()
        for nxt in ((3,), (4, 2), (5,))[i]:
            w_copy(nxt, k).start()

    def w_steps(*names):
        for name in names:
            i, k = "xzdXZD".index(name[0]), int(name[1:])
            if i < 3:
                w_copy(i, k).start()
            else:
                forward(i - 3, k)

    w_steps(*PLAN["near"])
    if not LATE:
        features(range(16, blk, 16))

    @pl.when(me < seq_count - 1)
    def _():
        rim_copy().start()

    def reach(dz):
        for to in (z + dz) * 2 + 1 - x, (z + dz) * 2 + x:
            spread(kv_own, kv_all, sem_kvm_s, sem_kvm_r, (to + seq_count - me) % seq_count, main).start()

    spread(kv_own, kv_all, sem_kvm_s, sem_kvm_r, (seq_count + 1 - 2 * x) % seq_count, main).start()
    for span in range(1, zn):
        if span > 1:
            hear(span - 1)
            if span < zn - 1:
                tell(span)
        for dz in (span, -span):
            pl.when(within(dz))(functools.partial(reach, dz))
    w_steps(*PLAN["kv"])

    load(5).wait()
    bands = modes.shape[0]
    band = lax.broadcasted_iota(jnp.int32, (bands, LANES), 0)
    mode = jnp.zeros((bands, LANES), jnp.int32)
    for b in range(bands):
        mode = jnp.where(band == b, modes[b], mode)
    mode = jnp.concatenate([mode] * (total // LANES), axis=1)
    steps = lax.broadcasted_iota(jnp.int32, (bands, total), 1)
    phase = (mode * steps) & (total - 1)
    turn_unit = f32(2.0 * math.pi / total)
    positional = sine(jnp.concatenate([phase + total // 4, phase], axis=0).astype(f32) * turn_unit)
    load(6).wait()
    hidden = sine(lax.dot_general(
        first[...], positional, (((0,), (0,)), ((), ())), precision=lax.Precision.HIGHEST,
        preferred_element_type=f32))
    load(7).wait()
    raw = lax.dot_general(
        hidden, filter_cols[...], (((0,), (0,)), ((), ())), precision=lax.Precision.HIGHEST,
        preferred_element_type=f32)
    load(8).wait()
    rate = decay[...]
    root = jnp.sqrt(2.0 * rate)
    pieces = []
    for r in range(seq_count):
        time = (lax.broadcasted_iota(jnp.int32, (blk, LANES), 0) + r * blk).astype(f32)
        pieces.append((root * jnp.exp(-rate * time) * raw[r * blk : (r + 1) * blk]).astype(bf16))
    now = jnp.concatenate(pieces, axis=1)
    before = jnp.concatenate([jnp.zeros((blk, LANES), bf16)] + pieces[:-1], axis=1)
    window = jnp.concatenate([before, now], axis=0)
    spectrum = jnp.dot(table[:size, :], window, preferred_element_type=f32) + jnp.dot(
        table[size : 2 * size, :], window, preferred_element_type=f32)
    row0 = lax.broadcasted_iota(jnp.int32, (blk, total), 0) == 0
    real, imag = spectrum[:blk], spectrum[blk:]
    spec_r[...] = real
    spec_i[...] = jnp.where(row0, 0.0, imag)
    spec_n[...] = jnp.where(row0, imag, real)

    @pl.when(me > 0)
    def _():
        rim_copy().wait_recv()
        for st in range(3):
            xt[st, 0:8, :] = rim_in[8 * st : 8 * st + 8, :].astype(f32)

    @pl.when(me == 0)
    def _():
        for st in range(3):
            xt[st, 0:8, :] = jnp.zeros((8, xt.shape[2]), f32)

    features((0,))
    for d in order:
        spread(kv_own, kv_all, sem_kvh_s, sem_kvh_r, d, top).start()
    w_steps(*PLAN["top"])
    for i, d in enumerate(order):
        if i >= QLAG:
            spread(kv_own, kv_all, sem_kvm_s, sem_kvm_r, order[i - QLAG], main).wait_send()
        spread(q_own, q_all, sem_q_s, sem_q_r, d, whole).start()
        w_steps(*PLAN["q"][i])
    kv_all[:, lane(me)] = kv_own[:, lane(me)]
    q_all[:, lane(me)] = q_own[:, lane(me)]

    for d in order:
        landing(kv_own, kv_all, sem_kvm_s, sem_kvm_r, d, main).wait_recv()
    for d in order:
        landing(kv_own, kv_all, sem_kvh_s, sem_kvh_r, d, top).wait_recv()
    w_steps(*PLAN["land"])
    kv = kv_all[...]
    spec_x[...] = jnp.dot(
        table[2 * size : 3 * size, :], jnp.concatenate([kv, kv], axis=0), preferred_element_type=f32)

    def product(i, carry):
        lo = pl.ds(pl.multiple_of(i * 16, 16), 16)
        hi = pl.ds(pl.multiple_of(blk + i * 16, 16), 16)
        for p in range(seq_count):
            y_real = y_imag = None
            for s in range(p + 1):
                sl, fl = pl.ds(s * LANES, LANES), pl.ds((p - s) * LANES, LANES)
                xr, xi = spec_x[lo, sl], spec_x[hi, sl]
                hr, him, hn = spec_r[lo, fl], spec_i[lo, fl], spec_n[lo, fl]
                tr = xr * hr - xi * him
                ti = xr * him + xi * hn
                y_real = tr if y_real is None else y_real + tr
                y_imag = ti if y_imag is None else y_imag + ti
            spec_y[lo, pl.ds(p * LANES, LANES)] = y_real.astype(bf16)
            spec_y[hi, pl.ds(p * LANES, LANES)] = y_imag.astype(bf16)
        return carry

    lax.fori_loop(0, blk // 16, product, 0)
    spec_r[...] = jnp.dot(table[3 * size : 3 * size + blk, :], spec_y[...], preferred_element_type=f32)
    w_steps(*PLAN["conv"])
    def rows_of(j):
        return pl.ds(pl.multiple_of(j * blk, blk), blk)

    def g_send(turn, d):
        to = (me + d) % seq_count
        far = to // groups
        rows = rows_of(1 - far if turn == 0 else far)
        return pltpu.make_async_remote_copy(
            src_ref=gate_own.at[to % groups, rows, :], dst_ref=gate_all.at[z, rows, lane(x)],
            send_sem=sem_g_s.at[turn, d], recv_sem=sem_g_r.at[turn, d], device_id=dev(to, core), device_id_type=MESH)

    def g_land(turn, d):
        source = (me + seq_count - d) % seq_count
        rows = rows_of(1 - side if turn == 0 else side)
        return pltpu.make_async_remote_copy(
            src_ref=gate_own.at[0, rows, :], dst_ref=gate_all.at[source // 2, rows, lane(source % 2)],
            send_sem=sem_g_s.at[turn, d], recv_sem=sem_g_r.at[turn, d], device_id=dev(source, core),
            device_id_type=MESH)

    load(9).wait()
    gain = skip[...]
    for i, d in enumerate((0, *order)):
        w_steps(*PLAN["gate"][i])
        if d:
            landing(q_own, q_all, sem_q_s, sem_q_r, d, whole).wait_recv()
        p = (me + seq_count - d) % seq_count
        sl = lane(p)
        inner = spec_r[:, sl].astype(bf16).astype(f32) + gain * kv_all[:, sl].astype(f32)
        gate_own[p % groups, rows_of(p // groups), :] = (q_all[:, sl].astype(f32) * inner).astype(bf16)
        if d != groups:
            g_send(0, (groups - d) % seq_count).start()
    w_steps(*PLAN["g0"])
    for i, d in enumerate(order):
        g_send(1, seq_count - d).start()
        w_steps(*PLAN["g1"][i])
    gate_all[z, :, lane(x)] = gate_own[group]
    load(10).wait()

    flip_x, flip_z = 1 - 2 * x, 2 - 4 * (z % 2)
    places = (group, group + flip_z, group + flip_x, group + flip_x + flip_z)
    slots = (None, 1, 0, 2)

    def project(j, first_turn, then):
        left = [gate_all[k, rows_of(j), :] for k in range(zn)]
        for i, (place, slot) in enumerate(zip(places, slots)):
            if first_turn:
                w_steps(*PLAN["far"][i])
            if slot is not None and first_turn:
                for k in range(CHUNKS):
                    w_back(slot, k).wait_recv()
            value = None
            for k in range(zn):
                deep = pl.ds(k * 2 * LANES, 2 * LANES)
                right = w_out[deep, :] if slot is None else w_next[slot, deep, :]
                term = jnp.dot(left[k], right, preferred_element_type=f32)
                value = term if value is None else value + term
            acc[rows_of(j), lane(place, cols)] = value
            then(place)

    def a_copy(i):
        return pltpu.make_async_remote_copy(
            src_ref=acc.at[rows_of(other), lane(i, cols)], dst_ref=acc_in.at[:, lane(i, cols)],
            send_sem=sem_a_s.at[i], recv_sem=sem_a_r.at[i], device_id=dev(me, other), device_id_type=MESH)

    def o_copy(i):
        return pltpu.make_async_remote_copy(
            src_ref=part.at[:, lane(i, cols)], dst_ref=out.at[:, lane(i, cols)],
            send_sem=sem_o_s.at[i], recv_sem=sem_o_r.at[i], device_id=dev(groups * core + group, side),
            device_id_type=MESH)

    for d in order:
        g_land(0, d).wait_recv()
    def give(place):
        a_copy(place).start()

    def take(place, store):
        a_copy(place).wait_recv()
        ln = lane(place, cols)
        store[:, ln] = (acc[rows_of(core), ln] + acc_in[:, ln]).astype(bf16)

    def far(place):
        pl.when(core == side)(lambda: give(place))

        @pl.when(core != side)
        def _():
            take(place, part)
            o_copy(place).start()

    def near(place):
        pl.when(core != side)(lambda: give(place))
        pl.when(core == side)(lambda: take(place, out))

    project(1 - side, True, far)
    for d in order:
        g_land(1, d).wait_recv()
    project(side, False, near)

    @pl.when(core != side)
    def _():
        for i in range(groups):
            o_copy(i).wait_recv()
            o_copy(i).wait_send()

    @pl.when(me < seq_count - 1)
    def _():
        rim_copy().wait_send()

    for d in order:
        spread(kv_own, kv_all, sem_kvh_s, sem_kvh_r, d, top).wait_send()
        spread(q_own, q_all, sem_q_s, sem_q_r, d, whole).wait_send()
        g_send(0, d).wait_send()
        g_send(1, d).wait_send()
    for d in order[max(0, len(order) - QLAG) :]:
        spread(kv_own, kv_all, sem_kvm_s, sem_kvm_r, d, main).wait_send()
    for i in range(6):
        for k in range(CHUNKS):
            w_copy(i, k).wait_send()
    for i in range(groups):
        a_copy(i).wait_send()


def fused(
    streams, short_weight, filter_modes, filter_first, filter_out, decay_rate, skip_gain, w_out
):
    f32, bf16 = jnp.float32, jnp.bfloat16
    n = lax.axis_size("seq")
    width, blk = streams.shape[1], streams.shape[2]
    cols = w_out.shape[1]
    total = n * blk
    dma = pltpu.SemaphoreType.DMA
    vmem = pltpu.VMEM
    return pl.pallas_call(
        functools.partial(mixer, n),
        out_shape=pltpu.VMEM((blk, n * cols // 2), bf16),
        in_specs=[
            pl.BlockSpec(memory_space=pltpu.HBM) for _ in range(9)
        ],
        out_specs=pl.BlockSpec(memory_space=pltpu.VMEM),
        scratch_shapes=[
            vmem(streams.shape, bf16),
            vmem(short_weight.shape, f32),
            pltpu.SMEM(filter_modes.shape, jnp.int32),
            vmem(filter_first.shape, f32),
            vmem((filter_out.shape[0], LANES), f32),
            vmem((1, LANES), f32),
            vmem((1, LANES), f32),
            vmem(w_out.shape, bf16),
            vmem((8 * blk, 2 * blk), bf16),
            vmem((3, 8 + blk, width), f32),
            vmem((24, width), bf16),
            vmem((24, width), bf16),
            vmem((blk, width), bf16),
            vmem((blk, width), bf16),
            vmem((blk, total), bf16),
            vmem((blk, total), bf16),
            vmem((2 * blk, total), f32),
            vmem((blk, total), f32),
            vmem((blk, total), f32),
            vmem((blk, total), f32),
            vmem((2 * blk, total), bf16),
            vmem((n // 2, 2 * blk, LANES), bf16),
            vmem((n // 2, 2 * blk, 2 * LANES), bf16),
            vmem((3, *w_out.shape), bf16),
            vmem((2 * blk, n // 2 * cols), f32),
            vmem((blk, n // 2 * cols), f32),
            vmem((blk, n // 2 * cols), bf16),
            pltpu.SemaphoreType.REGULAR((2, 2)),
            dma((11,)),
            dma((2,)),
            dma((n,)), dma((n,)),
            dma((n,)), dma((n,)),
            dma((n,)), dma((n,)),
            dma((2, n)), dma((2, n)),
            dma((6, CHUNKS)), dma((6, CHUNKS)),
            dma((n // 2,)), dma((n // 2,)),
            dma((n // 2,)), dma((n // 2,)),
        ],
        compiler_params=pltpu.CompilerParams(
            collective_id=0, has_side_effects=True, vmem_limit_bytes=56 * 1024 * 1024
        ),
    )(
        streams, short_weight, filter_modes, filter_first, filter_out,
        decay_rate.reshape(1, -1), skip_gain.reshape(1, -1), w_out, jnp.asarray(tables(blk)),
    )


def plan(
    streams, short_weight, filter_modes, filter_first, filter_out, decay_rate, skip_gain, w_out
):
    n = lax.axis_size("seq")
    width, blk = streams.shape[1], streams.shape[2]
    fits = n == 8 and lax.axis_size("chan") == 2 and lax.axis_size("grp") == 2 and blk == LANES and width == n * LANES
    fits = fits and short_weight.shape[1] <= 9 and w_out.shape[1] % LANES == 0
    form = fused if fits else local
    return form(
        streams, short_weight, filter_modes, filter_first, filter_out, decay_rate, skip_gain, w_out
    )


def solution(mesh):
    return jax.shard_map(
        plan,
        mesh=mesh,
        in_specs=(
            P(None, "chan", ("grp", "seq")),
            P(None, None, "chan"),
            P(),
            P(),
            P(None, "chan"),
            P("chan"),
            P("chan"),
            P("chan", "seq"),
        ),
        out_specs=P(("grp", "seq"), "chan"),
        check_vma=False,
    )
```

```python
import functools
import math

import jax
import jax.numpy as jnp
import numpy as np
from jax import lax
from jax.experimental import pallas as pl
from jax.experimental.pallas import tpu as pltpu
from jax.sharding import PartitionSpec as P


def shifted(value, axis, steps):
    count = lax.axis_size(axis)
    leading, last = (max(0, -steps), min(count, count - steps))
    return lax.ppermute(value, axis, [(source, source + steps) for source in range(leading, last)])


def position_filter(
    positions, mode_ints, first_layer, out_cols, decay_rates, tokens_dev, seq_count
):
    total_len = tokens_dev * seq_count
    block_idx = positions // tokens_dev
    offset_idx = positions % tokens_dev
    upper_part = mode_ints[:, None] * block_idx[None, :] % seq_count
    lower_part = mode_ints[:, None] * offset_idx[None, :] % total_len
    phase_int = (tokens_dev * upper_part + lower_part) % total_len
    phase_angle = phase_int.astype(jnp.float32) * jnp.float32(2.0 * math.pi / total_len)
    features = jnp.concatenate([jnp.cos(phase_angle), jnp.sin(phase_angle)], axis=0)
    hidden = jnp.sin(
        jnp.dot(
            first_layer.T,
            features,
            precision=lax.Precision.HIGHEST,
            preferred_element_type=jnp.float32,
        )
    )
    raw_values = jnp.dot(
        out_cols.T, hidden, precision=lax.Precision.HIGHEST, preferred_element_type=jnp.float32
    )
    time_float = positions.astype(jnp.float32)
    scaled = (
        jnp.sqrt(2.0 * decay_rates)[:, None]
        * jnp.exp(-decay_rates[:, None] * time_float[None, :])
        * raw_values
    )
    return scaled.astype(jnp.bfloat16)


def angle_table(rows_count, cols_count, modulus):
    product = (
        jnp.arange(rows_count, dtype=jnp.int32)[:, None]
        * jnp.arange(cols_count, dtype=jnp.int32)[None, :]
        % modulus
    )
    phase_angle = product.astype(jnp.float32) * jnp.float32(2.0 * math.pi / modulus)
    return (jnp.cos(phase_angle), jnp.sin(phase_angle))


def contract(form, left, right):
    return jnp.einsum(
        form, left, right, precision=lax.Precision.HIGHEST, preferred_element_type=jnp.float32
    )


def local(
    streams, short_weight, filter_modes, filter_first, filter_out, decay_rate, skip_gain, w_out
):
    seq_count = lax.axis_size("seq")
    seq_index = lax.axis_index("seq")
    width_half = streams.shape[1]
    tokens_dev = streams.shape[2]
    reach = short_weight.shape[1] - 1
    per_device = width_half // seq_count
    total_len = tokens_dev * seq_count
    rim = shifted(streams[:, :, tokens_dev - reach :], "seq", 1)
    extended = jnp.concatenate([rim, streams], axis=2).astype(jnp.float32)
    feature = short_weight[:, 0, :, None] * extended[:, :, reach:]
    for tap_index in range(1, reach + 1):
        feature = (
            feature
            + short_weight[:, tap_index, :, None]
            * extended[:, :, reach - tap_index : reach - tap_index + tokens_dev]
        )
    query = feature[0].astype(jnp.bfloat16)
    kv_product = (feature[1] * feature[2]).astype(jnp.bfloat16)
    positions = seq_index * tokens_dev + jnp.arange(tokens_dev, dtype=jnp.int32)
    filter_local = position_filter(
        positions, filter_modes, filter_first, filter_out, decay_rate, tokens_dev, seq_count
    )
    kv_channels, filter_channels = (
        lax.all_to_all(kv_product, "seq", split_axis=0, concat_axis=1, tiled=True),
        lax.all_to_all(filter_local, "seq", split_axis=0, concat_axis=1, tiled=True),
    )
    doubled = 2 * seq_count
    padded_len = 2 * total_len
    cos_outer, sin_outer = angle_table(doubled, seq_count, doubled)
    cos_twist, sin_twist = angle_table(doubled, tokens_dev, padded_len)
    cos_inner, sin_inner = angle_table(tokens_dev, tokens_dev, tokens_dev)

    def forward(signal):
        shaped = signal.astype(jnp.float32).reshape(per_device, seq_count, tokens_dev)
        a_real = contract("cpj,kp->ckj", shaped, cos_outer)
        a_imag = -contract("cpj,kp->ckj", shaped, sin_outer)
        r_real = a_real * cos_twist + a_imag * sin_twist
        r_imag = a_imag * cos_twist - a_real * sin_twist
        x_real = contract("ckj,jm->ckm", r_real, cos_inner) + contract(
            "ckj,jm->ckm", r_imag, sin_inner
        )
        x_imag = contract("ckj,jm->ckm", r_imag, cos_inner) - contract(
            "ckj,jm->ckm", r_real, sin_inner
        )
        return (x_real, x_imag)

    kv_real, kv_imag = forward(kv_channels)
    fl_real, fl_imag = forward(filter_channels)
    y_real = kv_real * fl_real - kv_imag * fl_imag
    y_imag = kv_real * fl_imag + kv_imag * fl_real
    b_real = contract("ckm,mj->ckj", y_real, cos_inner) - contract("ckm,mj->ckj", y_imag, sin_inner)
    b_imag = contract("ckm,mj->ckj", y_imag, cos_inner) + contract("ckm,mj->ckj", y_real, sin_inner)
    t_real = b_real * cos_twist - b_imag * sin_twist
    t_imag = b_real * sin_twist + b_imag * cos_twist
    conv_values = contract("ckj,kp->cpj", t_real, cos_outer) - contract(
        "ckj,kp->cpj", t_imag, sin_outer
    )
    conv_channels = (
        (conv_values * jnp.float32(1.0 / padded_len))
        .reshape(per_device, total_len)
        .astype(jnp.bfloat16)
    )
    conv_tokens = lax.all_to_all(conv_channels, "seq", split_axis=1, concat_axis=0, tiled=True)
    gated = (
        query.astype(jnp.float32)
        * (conv_tokens.astype(jnp.float32) + skip_gain[:, None] * kv_product.astype(jnp.float32))
    ).astype(jnp.bfloat16)
    partial_out = lax.dot_general(
        gated,
        lax.all_gather(w_out, "seq", axis=1, tiled=True),
        (((0,), (0,)), ((), ())),
        preferred_element_type=jnp.float32,
    )
    return lax.psum_scatter(partial_out, "chan", scatter_dimension=1, tiled=True).astype(
        jnp.bfloat16
    )


LANES = 128
CHUNKS = 4
QLAG = 7
LATE = False
PLAN = {'near': ('z0', 'x0', 'z1', 'x1'), 'mid': (), 'kv': ('x2', 'x3'), 'top': (), 'q': ((), (), (), (), (), (), ('z2', 'z3', 'X0', 'Z0', 'X1', 'Z1')), 'land': (), 'conv': ('X2', 'Z2'), 'gate': ((), (), (), (), (), (), (), ()), 'g0': (), 'g1': ((), (), (), (), (), (), ('X3', 'D0', 'Z3', 'D1', 'D2', 'D3')), 'far': ((), (), (), ())}
MESH = pl.DeviceIdType.MESH


def tables(block):
    size = 2 * block
    steps = np.arange(size)
    angle = 2.0 * np.pi * (np.outer(np.arange(block), steps) % size) / size
    forward = np.concatenate([np.cos(angle), -np.sin(angle)], axis=0)
    forward[block] = np.cos(np.pi * steps)
    weight = np.full((size, 1), 2.0 / size)
    weight[0] = weight[block] = 1.0 / size
    inverse = (forward * weight).T[block:]
    upper = np.asarray(forward, dtype=jnp.bfloat16)
    lower = np.asarray(forward - upper.astype(np.float64), dtype=jnp.bfloat16)
    both = np.concatenate([upper[:, :block], lower[:, :block]], axis=1)
    unit = np.eye(block, size)
    return np.concatenate(
        [upper, lower, both, np.asarray(inverse, jnp.bfloat16), np.asarray(unit, jnp.bfloat16)], axis=0
    )


def split_pi():
    parts, rest = [], math.pi
    for bits in (10, 22):
        part = math.floor(rest * 2.0**bits) / 2.0**bits
        parts.append(part)
        rest -= part
    return (*parts, rest)


def sine(value):
    f32 = jnp.float32
    count = jnp.floor(value * f32(1.0 / math.pi) + f32(0.5))
    rest = value
    for part in split_pi():
        rest = rest - count * f32(part)
    half = count * f32(0.5)
    sign = f32(1.0) - f32(4.0) * (half - jnp.floor(half))
    square = rest * rest
    series = f32(0.0)
    for degree in range(13, 1, -2):
        series = (series + f32((-1.0) ** (degree // 2) / math.factorial(degree))) * square
    return sign * (rest + rest * series)


def mixer(
    seq_count, streams_h, short_h, modes_h, first_h, filter_h, decay_h, skip_h, w_h, table_h, out,
    streams, short_weight, modes, first, filter_cols, decay, skip, w_out, table,
    xt, rim_out, rim_in, kv_own, q_own, kv_all, q_all, spec_x, spec_r, spec_i, spec_n, spec_y,
    gate_own, gate_all, w_next, acc, acc_in, part,
    sem_far, sem_in, sem_rim, sem_kvm_s, sem_kvm_r, sem_kvh_s, sem_kvh_r, sem_q_s, sem_q_r, sem_g_s, sem_g_r,
    sem_w_s, sem_w_r, sem_a_s, sem_a_r, sem_o_s, sem_o_r,
):
    f32, bf16 = jnp.float32, jnp.bfloat16
    blk = streams.shape[2]
    size = 2 * blk
    taps = short_weight.shape[1]
    total = seq_count * blk
    cols = w_out.shape[1]
    zn = seq_count // 2
    groups = seq_count // 2
    grp = lax.axis_index("grp")
    me = lax.axis_index("seq")
    core = lax.axis_index("chan")
    other = 1 - core
    z = me // 2
    x = me % 2
    side = me // groups
    group = me % groups

    def dev(seq, chan):
        return (grp, seq, chan)

    def lane(i, n=LANES):
        return pl.ds(pl.multiple_of(i * n, n), n)

    barrier = pltpu.get_barrier_semaphore()
    def within(dz):
        return jnp.logical_and(z + dz >= 0, z + dz < zn)

    def hello(to):
        pl.semaphore_signal(barrier, inc=1, device_id=to, device_id_type=MESH)

    for dz in (1, -1):

        @pl.when(within(dz))
        def _():
            for px in range(2):
                for ch in (core, other):
                    hello(dev((z + dz) * 2 + px, ch))

    for near in (dev(z * 2 + 1 - x, core), dev(z * 2 + 1 - x, other), dev(me, other), (1 - grp, me, core)):
        hello(near)

    def tell(level):
        for i, dz in enumerate((1, -1)):

            @pl.when(jnp.logical_and(within(-dz), within(dz * level)))
            def _():
                pl.semaphore_signal(
                    sem_far.at[level - 1, i], inc=1, device_id=dev(me - 2 * dz, core), device_id_type=MESH)

    def hear(level):
        for i, dz in enumerate((1, -1)):

            @pl.when(within(dz * (level + 1)))
            def _():
                pl.semaphore_wait(sem_far.at[level - 1, i], 1)

    here = lane(me)
    loads = (
        (table_h, table),
        (streams_h.at[0], streams.at[0]),
        (streams_h.at[1], streams.at[1]),
        (streams_h.at[2], streams.at[2]),
        (short_h, short_weight),
        (modes_h, modes),
        (first_h, first),
        (filter_h.at[:, here], filter_cols),
        (decay_h.at[:, here], decay),
        (skip_h.at[:, here], skip),
        (w_h, w_out),
    )

    def load(i):
        return pltpu.make_async_copy(loads[i][0], loads[i][1], sem_in.at[i])

    for i in range(len(loads)):
        load(i).start()
    load(0).wait()
    eye = table[4 * blk + 2 * blk + blk : 4 * blk + 2 * blk + 2 * blk, :blk]
    for st in range(3):
        load(1 + st).wait()
        turned = lax.dot_general(eye, streams[st], (((1,), (1,)), ((), ())), preferred_element_type=f32)
        xt[st, 8:, :] = turned
    rim_out[...] = jnp.concatenate([xt[st, blk:, :] for st in range(3)], axis=0).astype(bf16)

    def features(rows):
        def body(l, carry):
            ln = lane(l)
            for r0 in rows:
                feat = []
                for st in range(3):
                    total_f = short_weight[st, pl.ds(0, 1), ln] * xt[st, pl.ds(8 + r0, 16), ln]
                    for i in range(1, taps):
                        total_f = total_f + short_weight[st, pl.ds(i, 1), ln] * xt[st, pl.ds(8 + r0 - i, 16), ln]
                    feat.append(total_f)
                q_own[pl.ds(r0, 16), ln] = feat[0].astype(bf16)
                kv_own[pl.ds(r0, 16), ln] = (feat[1] * feat[2]).astype(bf16)
            return carry

        lax.fori_loop(0, seq_count, body, 0)

    load(4).wait()
    if LATE:
        features(range(16, blk, 16))
    inner = jnp.logical_and(within(1), within(-1))
    pl.when(inner)(lambda: pl.semaphore_wait(barrier, 12))
    pl.when(jnp.logical_not(inner))(lambda: pl.semaphore_wait(barrier, 8))
    tell(1)

    def rim_copy():
        return pltpu.make_async_remote_copy(
            src_ref=rim_out, dst_ref=rim_in, send_sem=sem_rim.at[0], recv_sem=sem_rim.at[1],
            device_id=dev((me + 1) % seq_count, core), device_id_type=MESH)

    def spread(own, every, send, recv, d, rows):
        to = (me + d) % seq_count
        return pltpu.make_async_remote_copy(
            src_ref=own.at[rows, lane(to)], dst_ref=every.at[rows, lane(me)],
            send_sem=send.at[d], recv_sem=recv.at[d], device_id=dev(to, core), device_id_type=MESH)

    def landing(own, every, send, recv, d, rows):
        source = (me + seq_count - d) % seq_count
        return pltpu.make_async_remote_copy(
            src_ref=own.at[rows, lane(source)], dst_ref=every.at[rows, lane(source)],
            send_sem=send.at[d], recv_sem=recv.at[d], device_id=dev(source, core), device_id_type=MESH)

    main, top, whole = pl.ds(16, blk - 16), pl.ds(0, 16), pl.ds(0, blk)
    order = (4, 3, 5, 2, 6, 1, 7) if seq_count == 8 else tuple(range(1, seq_count))

    part_rows = w_out.shape[0] // 2
    step_rows = part_rows // CHUNKS
    beside = dev(me + 1 - 2 * x, core)
    above = dev(me + 2 - 4 * (z % 2), core)
    across = (1 - grp, me, core)
    w_source = (w_h, w_h, w_next.at[1], w_next.at[0], w_next.at[1], w_next.at[2])
    w_slot = (0, 1, 2, 0, 1, 2)
    w_to = (beside, above, beside, across, across, across)

    def chunk(side_y, k):
        return pl.ds(pl.multiple_of(side_y * part_rows + k * step_rows, step_rows), step_rows)

    def w_copy(i, k):
        return pltpu.make_async_remote_copy(
            src_ref=w_source[i].at[chunk(grp, k), :], dst_ref=w_next.at[w_slot[i], chunk(grp, k), :],
            send_sem=sem_w_s.at[i, k], recv_sem=sem_w_r.at[i, k], device_id=w_to[i], device_id_type=MESH)

    def w_back(slot, k):
        return pltpu.make_async_remote_copy(
            src_ref=w_next.at[slot, chunk(1 - grp, k), :], dst_ref=w_next.at[slot, chunk(1 - grp, k), :],
            send_sem=sem_w_s.at[3 + slot, k], recv_sem=sem_w_r.at[3 + slot, k], device_id=across, device_id_type=MESH)

    def forward(i, k):
        w_copy(i, k).wait_recv()
        for nxt in ((3,), (4, 2), (5,))[i]:
            w_copy(nxt, k).start()

    def w_steps(*names):
        for name in names:
            i, k = "xzdXZD".index(name[0]), int(name[1:])
            if i < 3:
                w_copy(i, k).start()
            else:
                forward(i - 3, k)

    w_steps(*PLAN["near"])
    if not LATE:
        features(range(16, blk, 16))

    @pl.when(me < seq_count - 1)
    def _():
        rim_copy().start()

    def reach(dz):
        for to in (z + dz) * 2 + 1 - x, (z + dz) * 2 + x:
            spread(kv_own, kv_all, sem_kvm_s, sem_kvm_r, (to + seq_count - me) % seq_count, main).start()

    spread(kv_own, kv_all, sem_kvm_s, sem_kvm_r, (seq_count + 1 - 2 * x) % seq_count, main).start()
    for span in range(1, zn):
        if span > 1:
            hear(span - 1)
            if span < zn - 1:
                tell(span)
        for dz in (span, -span):
            pl.when(within(dz))(functools.partial(reach, dz))
    w_steps(*PLAN["kv"])

    load(5).wait()
    bands = modes.shape[0]
    band = lax.broadcasted_iota(jnp.int32, (bands, LANES), 0)
    mode = jnp.zeros((bands, LANES), jnp.int32)
    for b in range(bands):
        mode = jnp.where(band == b, modes[b], mode)
    mode = jnp.concatenate([mode] * (total // LANES), axis=1)
    steps = lax.broadcasted_iota(jnp.int32, (bands, total), 1)
    phase = (mode * steps) & (total - 1)
    turn_unit = f32(2.0 * math.pi / total)
    positional = sine(jnp.concatenate([phase + total // 4, phase], axis=0).astype(f32) * turn_unit)
    load(6).wait()
    hidden = sine(lax.dot_general(
        first[...], positional, (((0,), (0,)), ((), ())), precision=lax.Precision.HIGHEST,
        preferred_element_type=f32))
    load(7).wait()
    raw = lax.dot_general(
        hidden, filter_cols[...], (((0,), (0,)), ((), ())), precision=lax.Precision.HIGHEST,
        preferred_element_type=f32)
    load(8).wait()
    rate = decay[...]
    root = jnp.sqrt(2.0 * rate)
    pieces = []
    for r in range(seq_count):
        time = (lax.broadcasted_iota(jnp.int32, (blk, LANES), 0) + r * blk).astype(f32)
        pieces.append((root * jnp.exp(-rate * time) * raw[r * blk : (r + 1) * blk]).astype(bf16))
    now = jnp.concatenate(pieces, axis=1)
    before = jnp.concatenate([jnp.zeros((blk, LANES), bf16)] + pieces[:-1], axis=1)
    window = jnp.concatenate([before, now], axis=0)
    spectrum = jnp.dot(table[:size, :], window, preferred_element_type=f32) + jnp.dot(
        table[size : 2 * size, :], window, preferred_element_type=f32)
    row0 = lax.broadcasted_iota(jnp.int32, (blk, total), 0) == 0
    real, imag = spectrum[:blk], spectrum[blk:]
    spec_r[...] = real
    spec_i[...] = jnp.where(row0, 0.0, imag)
    spec_n[...] = jnp.where(row0, imag, real)

    @pl.when(me > 0)
    def _():
        rim_copy().wait_recv()
        for st in range(3):
            xt[st, 0:8, :] = rim_in[8 * st : 8 * st + 8, :].astype(f32)

    @pl.when(me == 0)
    def _():
        for st in range(3):
            xt[st, 0:8, :] = jnp.zeros((8, xt.shape[2]), f32)

    features((0,))
    for d in order:
        spread(kv_own, kv_all, sem_kvh_s, sem_kvh_r, d, top).start()
    w_steps(*PLAN["top"])
    for i, d in enumerate(order):
        if i >= QLAG:
            spread(kv_own, kv_all, sem_kvm_s, sem_kvm_r, order[i - QLAG], main).wait_send()
        spread(q_own, q_all, sem_q_s, sem_q_r, d, whole).start()
        w_steps(*PLAN["q"][i])
    kv_all[:, lane(me)] = kv_own[:, lane(me)]
    q_all[:, lane(me)] = q_own[:, lane(me)]

    for d in order:
        landing(kv_own, kv_all, sem_kvm_s, sem_kvm_r, d, main).wait_recv()
    for d in order:
        landing(kv_own, kv_all, sem_kvh_s, sem_kvh_r, d, top).wait_recv()
    w_steps(*PLAN["land"])
    kv = kv_all[...]
    spec_x[...] = jnp.dot(
        table[2 * size : 3 * size, :], jnp.concatenate([kv, kv], axis=0), preferred_element_type=f32)

    def product(i, carry):
        lo = pl.ds(pl.multiple_of(i * 16, 16), 16)
        hi = pl.ds(pl.multiple_of(blk + i * 16, 16), 16)
        for p in range(seq_count):
            y_real = y_imag = None
            for s in range(p + 1):
                sl, fl = pl.ds(s * LANES, LANES), pl.ds((p - s) * LANES, LANES)
                xr, xi = spec_x[lo, sl], spec_x[hi, sl]
                hr, him, hn = spec_r[lo, fl], spec_i[lo, fl], spec_n[lo, fl]
                tr = xr * hr - xi * him
                ti = xr * him + xi * hn
                y_real = tr if y_real is None else y_real + tr
                y_imag = ti if y_imag is None else y_imag + ti
            spec_y[lo, pl.ds(p * LANES, LANES)] = y_real.astype(bf16)
            spec_y[hi, pl.ds(p * LANES, LANES)] = y_imag.astype(bf16)
        return carry

    lax.fori_loop(0, blk // 16, product, 0)
    spec_r[...] = jnp.dot(table[3 * size : 3 * size + blk, :], spec_y[...], preferred_element_type=f32)
    w_steps(*PLAN["conv"])
    def rows_of(j):
        return pl.ds(pl.multiple_of(j * blk, blk), blk)

    def g_send(turn, d):
        to = (me + d) % seq_count
        far = to // groups
        rows = rows_of(1 - far if turn == 0 else far)
        return pltpu.make_async_remote_copy(
            src_ref=gate_own.at[to % groups, rows, :], dst_ref=gate_all.at[z, rows, lane(x)],
            send_sem=sem_g_s.at[turn, d], recv_sem=sem_g_r.at[turn, d], device_id=dev(to, core), device_id_type=MESH)

    def g_land(turn, d):
        source = (me + seq_count - d) % seq_count
        rows = rows_of(1 - side if turn == 0 else side)
        return pltpu.make_async_remote_copy(
            src_ref=gate_own.at[0, rows, :], dst_ref=gate_all.at[source // 2, rows, lane(source % 2)],
            send_sem=sem_g_s.at[turn, d], recv_sem=sem_g_r.at[turn, d], device_id=dev(source, core),
            device_id_type=MESH)

    load(9).wait()
    gain = skip[...]
    for i, d in enumerate((0, *order)):
        w_steps(*PLAN["gate"][i])
        if d:
            landing(q_own, q_all, sem_q_s, sem_q_r, d, whole).wait_recv()
        p = (me + seq_count - d) % seq_count
        sl = lane(p)
        inner = spec_r[:, sl].astype(bf16).astype(f32) + gain * kv_all[:, sl].astype(f32)
        gate_own[p % groups, rows_of(p // groups), :] = (q_all[:, sl].astype(f32) * inner).astype(bf16)
        if d != groups:
            g_send(0, (groups - d) % seq_count).start()
    w_steps(*PLAN["g0"])
    for i, d in enumerate(order):
        g_send(1, seq_count - d).start()
        w_steps(*PLAN["g1"][i])
    gate_all[z, :, lane(x)] = gate_own[group]
    load(10).wait()

    flip_x, flip_z = 1 - 2 * x, 2 - 4 * (z % 2)
    places = (group, group + flip_z, group + flip_x, group + flip_x + flip_z)
    slots = (None, 1, 0, 2)

    def project(j, first_turn, then):
        left = [gate_all[k, rows_of(j), :] for k in range(zn)]
        for i, (place, slot) in enumerate(zip(places, slots)):
            if first_turn:
                w_steps(*PLAN["far"][i])
            if slot is not None and first_turn:
                for k in range(CHUNKS):
                    w_back(slot, k).wait_recv()
            value = None
            for k in range(zn):
                deep = pl.ds(k * 2 * LANES, 2 * LANES)
                right = w_out[deep, :] if slot is None else w_next[slot, deep, :]
                term = jnp.dot(left[k], right, preferred_element_type=f32)
                value = term if value is None else value + term
            acc[rows_of(j), lane(place, cols)] = value
            then(place)

    def a_copy(i):
        return pltpu.make_async_remote_copy(
            src_ref=acc.at[rows_of(other), lane(i, cols)], dst_ref=acc_in.at[:, lane(i, cols)],
            send_sem=sem_a_s.at[i], recv_sem=sem_a_r.at[i], device_id=dev(me, other), device_id_type=MESH)

    def o_copy(i):
        return pltpu.make_async_remote_copy(
            src_ref=part.at[:, lane(i, cols)], dst_ref=out.at[:, lane(i, cols)],
            send_sem=sem_o_s.at[i], recv_sem=sem_o_r.at[i], device_id=dev(groups * core + group, side),
            device_id_type=MESH)

    for d in order:
        g_land(0, d).wait_recv()
    def give(place):
        a_copy(place).start()

    def take(place, store):
        a_copy(place).wait_recv()
        ln = lane(place, cols)
        store[:, ln] = (acc[rows_of(core), ln] + acc_in[:, ln]).astype(bf16)

    def far(place):
        pl.when(core == side)(lambda: give(place))

        @pl.when(core != side)
        def _():
            take(place, part)
            o_copy(place).start()

    def near(place):
        pl.when(core != side)(lambda: give(place))
        pl.when(core == side)(lambda: take(place, out))

    project(1 - side, True, far)
    for d in order:
        g_land(1, d).wait_recv()
    project(side, False, near)

    @pl.when(core != side)
    def _():
        for i in range(groups):
            o_copy(i).wait_recv()
            o_copy(i).wait_send()

    @pl.when(me < seq_count - 1)
    def _():
        rim_copy().wait_send()

    for d in order:
        spread(kv_own, kv_all, sem_kvh_s, sem_kvh_r, d, top).wait_send()
        spread(q_own, q_all, sem_q_s, sem_q_r, d, whole).wait_send()
        g_send(0, d).wait_send()
        g_send(1, d).wait_send()
    for d in order[max(0, len(order) - QLAG) :]:
        spread(kv_own, kv_all, sem_kvm_s, sem_kvm_r, d, main).wait_send()
    for i in range(6):
        for k in range(CHUNKS):
            w_copy(i, k).wait_send()
    for i in range(groups):
        a_copy(i).wait_send()


def fused(
    streams, short_weight, filter_modes, filter_first, filter_out, decay_rate, skip_gain, w_out
):
    f32, bf16 = jnp.float32, jnp.bfloat16
    n = lax.axis_size("seq")
    width, blk = streams.shape[1], streams.shape[2]
    cols = w_out.shape[1]
    total = n * blk
    dma = pltpu.SemaphoreType.DMA
    vmem = pltpu.VMEM
    return pl.pallas_call(
        functools.partial(mixer, n),
        out_shape=pltpu.VMEM((blk, n * cols // 2), bf16),
        in_specs=[
            pl.BlockSpec(memory_space=pltpu.HBM) for _ in range(9)
        ],
        out_specs=pl.BlockSpec(memory_space=pltpu.VMEM),
        scratch_shapes=[
            vmem(streams.shape, bf16),
            vmem(short_weight.shape, f32),
            pltpu.SMEM(filter_modes.shape, jnp.int32),
            vmem(filter_first.shape, f32),
            vmem((filter_out.shape[0], LANES), f32),
            vmem((1, LANES), f32),
            vmem((1, LANES), f32),
            vmem(w_out.shape, bf16),
            vmem((8 * blk, 2 * blk), bf16),
            vmem((3, 8 + blk, width), f32),
            vmem((24, width), bf16),
            vmem((24, width), bf16),
            vmem((blk, width), bf16),
            vmem((blk, width), bf16),
            vmem((blk, total), bf16),
            vmem((blk, total), bf16),
            vmem((2 * blk, total), f32),
            vmem((blk, total), f32),
            vmem((blk, total), f32),
            vmem((blk, total), f32),
            vmem((2 * blk, total), bf16),
            vmem((n // 2, 2 * blk, LANES), bf16),
            vmem((n // 2, 2 * blk, 2 * LANES), bf16),
            vmem((3, *w_out.shape), bf16),
            vmem((2 * blk, n // 2 * cols), f32),
            vmem((blk, n // 2 * cols), f32),
            vmem((blk, n // 2 * cols), bf16),
            pltpu.SemaphoreType.REGULAR((2, 2)),
            dma((11,)),
            dma((2,)),
            dma((n,)), dma((n,)),
            dma((n,)), dma((n,)),
            dma((n,)), dma((n,)),
            dma((2, n)), dma((2, n)),
            dma((6, CHUNKS)), dma((6, CHUNKS)),
            dma((n // 2,)), dma((n // 2,)),
            dma((n // 2,)), dma((n // 2,)),
        ],
        compiler_params=pltpu.CompilerParams(
            collective_id=0, has_side_effects=True, vmem_limit_bytes=56 * 1024 * 1024
        ),
    )(
        streams, short_weight, filter_modes, filter_first, filter_out,
        decay_rate.reshape(1, -1), skip_gain.reshape(1, -1), w_out, jnp.asarray(tables(blk)),
    )


def plan(
    streams, short_weight, filter_modes, filter_first, filter_out, decay_rate, skip_gain, w_out
):
    n = lax.axis_size("seq")
    width, blk = streams.shape[1], streams.shape[2]
    fits = n == 8 and lax.axis_size("chan") == 2 and lax.axis_size("grp") == 2 and blk == LANES and width == n * LANES
    fits = fits and short_weight.shape[1] <= 9 and w_out.shape[1] % LANES == 0
    form = fused if fits else local
    return form(
        streams, short_weight, filter_modes, filter_first, filter_out, decay_rate, skip_gain, w_out
    )


def solution(mesh):
    return jax.shard_map(
        plan,
        mesh=mesh,
        in_specs=(
            P(None, "chan", ("grp", "seq")),
            P(None, None, "chan"),
            P(),
            P(),
            P(None, "chan"),
            P("chan"),
            P("chan"),
            P("chan", "seq"),
        ),
        out_specs=P(("grp", "seq"), "chan"),
        check_vma=False,
    )
```

```python
import functools
import math

import jax
import jax.numpy as jnp
import numpy as np
from jax import lax
from jax.experimental import pallas as pl
from jax.experimental.pallas import tpu as pltpu
from jax.sharding import PartitionSpec as P


def shifted(value, axis, steps):
    count = lax.axis_size(axis)
    leading, last = (max(0, -steps), min(count, count - steps))
    return lax.ppermute(value, axis, [(source, source + steps) for source in range(leading, last)])


def position_filter(
    positions, mode_ints, first_layer, out_cols, decay_rates, tokens_dev, seq_count
):
    total_len = tokens_dev * seq_count
    block_idx = positions // tokens_dev
    offset_idx = positions % tokens_dev
    upper_part = mode_ints[:, None] * block_idx[None, :] % seq_count
    lower_part = mode_ints[:, None] * offset_idx[None, :] % total_len
    phase_int = (tokens_dev * upper_part + lower_part) % total_len
    phase_angle = phase_int.astype(jnp.float32) * jnp.float32(2.0 * math.pi / total_len)
    features = jnp.concatenate([jnp.cos(phase_angle), jnp.sin(phase_angle)], axis=0)
    hidden = jnp.sin(
        jnp.dot(
            first_layer.T,
            features,
            precision=lax.Precision.HIGHEST,
            preferred_element_type=jnp.float32,
        )
    )
    raw_values = jnp.dot(
        out_cols.T, hidden, precision=lax.Precision.HIGHEST, preferred_element_type=jnp.float32
    )
    time_float = positions.astype(jnp.float32)
    scaled = (
        jnp.sqrt(2.0 * decay_rates)[:, None]
        * jnp.exp(-decay_rates[:, None] * time_float[None, :])
        * raw_values
    )
    return scaled.astype(jnp.bfloat16)


def angle_table(rows_count, cols_count, modulus):
    product = (
        jnp.arange(rows_count, dtype=jnp.int32)[:, None]
        * jnp.arange(cols_count, dtype=jnp.int32)[None, :]
        % modulus
    )
    phase_angle = product.astype(jnp.float32) * jnp.float32(2.0 * math.pi / modulus)
    return (jnp.cos(phase_angle), jnp.sin(phase_angle))


def contract(form, left, right):
    return jnp.einsum(
        form, left, right, precision=lax.Precision.HIGHEST, preferred_element_type=jnp.float32
    )


def local(
    streams, short_weight, filter_modes, filter_first, filter_out, decay_rate, skip_gain, w_out
):
    seq_count = lax.axis_size("seq")
    seq_index = lax.axis_index("seq")
    width_half = streams.shape[1]
    tokens_dev = streams.shape[2]
    reach = short_weight.shape[1] - 1
    per_device = width_half // seq_count
    total_len = tokens_dev * seq_count
    rim = shifted(streams[:, :, tokens_dev - reach :], "seq", 1)
    extended = jnp.concatenate([rim, streams], axis=2).astype(jnp.float32)
    feature = short_weight[:, 0, :, None] * extended[:, :, reach:]
    for tap_index in range(1, reach + 1):
        feature = (
            feature
            + short_weight[:, tap_index, :, None]
            * extended[:, :, reach - tap_index : reach - tap_index + tokens_dev]
        )
    query = feature[0].astype(jnp.bfloat16)
    kv_product = (feature[1] * feature[2]).astype(jnp.bfloat16)
    positions = seq_index * tokens_dev + jnp.arange(tokens_dev, dtype=jnp.int32)
    filter_local = position_filter(
        positions, filter_modes, filter_first, filter_out, decay_rate, tokens_dev, seq_count
    )
    kv_channels, filter_channels = (
        lax.all_to_all(kv_product, "seq", split_axis=0, concat_axis=1, tiled=True),
        lax.all_to_all(filter_local, "seq", split_axis=0, concat_axis=1, tiled=True),
    )
    doubled = 2 * seq_count
    padded_len = 2 * total_len
    cos_outer, sin_outer = angle_table(doubled, seq_count, doubled)
    cos_twist, sin_twist = angle_table(doubled, tokens_dev, padded_len)
    cos_inner, sin_inner = angle_table(tokens_dev, tokens_dev, tokens_dev)

    def forward(signal):
        shaped = signal.astype(jnp.float32).reshape(per_device, seq_count, tokens_dev)
        a_real = contract("cpj,kp->ckj", shaped, cos_outer)
        a_imag = -contract("cpj,kp->ckj", shaped, sin_outer)
        r_real = a_real * cos_twist + a_imag * sin_twist
        r_imag = a_imag * cos_twist - a_real * sin_twist
        x_real = contract("ckj,jm->ckm", r_real, cos_inner) + contract(
            "ckj,jm->ckm", r_imag, sin_inner
        )
        x_imag = contract("ckj,jm->ckm", r_imag, cos_inner) - contract(
            "ckj,jm->ckm", r_real, sin_inner
        )
        return (x_real, x_imag)

    kv_real, kv_imag = forward(kv_channels)
    fl_real, fl_imag = forward(filter_channels)
    y_real = kv_real * fl_real - kv_imag * fl_imag
    y_imag = kv_real * fl_imag + kv_imag * fl_real
    b_real = contract("ckm,mj->ckj", y_real, cos_inner) - contract("ckm,mj->ckj", y_imag, sin_inner)
    b_imag = contract("ckm,mj->ckj", y_imag, cos_inner) + contract("ckm,mj->ckj", y_real, sin_inner)
    t_real = b_real * cos_twist - b_imag * sin_twist
    t_imag = b_real * sin_twist + b_imag * cos_twist
    conv_values = contract("ckj,kp->cpj", t_real, cos_outer) - contract(
        "ckj,kp->cpj", t_imag, sin_outer
    )
    conv_channels = (
        (conv_values * jnp.float32(1.0 / padded_len))
        .reshape(per_device, total_len)
        .astype(jnp.bfloat16)
    )
    conv_tokens = lax.all_to_all(conv_channels, "seq", split_axis=1, concat_axis=0, tiled=True)
    gated = (
        query.astype(jnp.float32)
        * (conv_tokens.astype(jnp.float32) + skip_gain[:, None] * kv_product.astype(jnp.float32))
    ).astype(jnp.bfloat16)
    partial_out = lax.dot_general(
        gated,
        lax.all_gather(w_out, "seq", axis=1, tiled=True),
        (((0,), (0,)), ((), ())),
        preferred_element_type=jnp.float32,
    )
    return lax.psum_scatter(partial_out, "chan", scatter_dimension=1, tiled=True).astype(
        jnp.bfloat16
    )


LANES = 128
CHUNKS = 4
QLAG = 7
LATE = False
EAGER = False
PLAN = {'near': ('z0', 'x0', 'z1', 'x1'), 'mid': (), 'kv': ('x2', 'x3'), 'top': (), 'q': ((), (), (), (), (), (), ('z2', 'z3', 'X0', 'Z0', 'X1', 'Z1', 'X2')), 'land': (), 'conv': ('Z2', 'X3'), 'gate': ((), (), (), (), (), (), (), ()), 'g0': (), 'g1': ((), (), (), (), (), (), ('D0', 'Z3', 'D1', 'D2', 'D3')), 'far': ((), (), (), ())}
MESH = pl.DeviceIdType.MESH


def tables(block):
    size = 2 * block
    steps = np.arange(size)
    angle = 2.0 * np.pi * (np.outer(np.arange(block), steps) % size) / size
    forward = np.concatenate([np.cos(angle), -np.sin(angle)], axis=0)
    forward[block] = np.cos(np.pi * steps)
    weight = np.full((size, 1), 2.0 / size)
    weight[0] = weight[block] = 1.0 / size
    inverse = (forward * weight).T[block:]
    upper = np.asarray(forward, dtype=jnp.bfloat16)
    lower = np.asarray(forward - upper.astype(np.float64), dtype=jnp.bfloat16)
    both = np.concatenate([upper[:, :block], lower[:, :block]], axis=1)
    unit = np.eye(block, size)
    return np.concatenate(
        [upper, lower, both, np.asarray(inverse, jnp.bfloat16), np.asarray(unit, jnp.bfloat16)], axis=0
    )


def split_pi():
    parts, rest = [], math.pi
    for bits in (10, 22):
        part = math.floor(rest * 2.0**bits) / 2.0**bits
        parts.append(part)
        rest -= part
    return (*parts, rest)


def sine(value):
    f32 = jnp.float32
    count = jnp.floor(value * f32(1.0 / math.pi) + f32(0.5))
    rest = value
    for part in split_pi():
        rest = rest - count * f32(part)
    half = count * f32(0.5)
    sign = f32(1.0) - f32(4.0) * (half - jnp.floor(half))
    square = rest * rest
    series = f32(0.0)
    for degree in range(13, 1, -2):
        series = (series + f32((-1.0) ** (degree // 2) / math.factorial(degree))) * square
    return sign * (rest + rest * series)


def mixer(
    seq_count, streams_h, short_h, modes_h, first_h, filter_h, decay_h, skip_h, w_h, table_h, out,
    streams, short_weight, modes, first, filter_cols, decay, skip, w_out, table,
    xt, rim_out, rim_in, kv_own, q_own, kv_all, q_all, spec_x, spec_r, spec_i, spec_n, spec_y,
    gate_own, gate_all, w_next, acc, acc_in, part,
    sem_far, sem_in, sem_rim, sem_kvm_s, sem_kvm_r, sem_kvh_s, sem_kvh_r, sem_q_s, sem_q_r, sem_g_s, sem_g_r,
    sem_w_s, sem_w_r, sem_a_s, sem_a_r, sem_o_s, sem_o_r,
):
    f32, bf16 = jnp.float32, jnp.bfloat16
    blk = streams.shape[2]
    size = 2 * blk
    taps = short_weight.shape[1]
    total = seq_count * blk
    cols = w_out.shape[1]
    zn = seq_count // 2
    groups = seq_count // 2
    grp = lax.axis_index("grp")
    me = lax.axis_index("seq")
    core = lax.axis_index("chan")
    other = 1 - core
    z = me // 2
    x = me % 2
    side = me // groups
    group = me % groups

    def dev(seq, chan):
        return (grp, seq, chan)

    def lane(i, n=LANES):
        return pl.ds(pl.multiple_of(i * n, n), n)

    barrier = pltpu.get_barrier_semaphore()
    def within(dz):
        return jnp.logical_and(z + dz >= 0, z + dz < zn)

    def hello(to):
        pl.semaphore_signal(barrier, inc=1, device_id=to, device_id_type=MESH)

    for dz in (1, -1):

        @pl.when(within(dz))
        def _():
            for px in range(2):
                for ch in (core, other):
                    hello(dev((z + dz) * 2 + px, ch))

    for near in (dev(z * 2 + 1 - x, core), dev(z * 2 + 1 - x, other), dev(me, other), (1 - grp, me, core)):
        hello(near)

    def tell(level):
        for i, dz in enumerate((1, -1)):

            @pl.when(jnp.logical_and(within(-dz), within(dz * level)))
            def _():
                pl.semaphore_signal(
                    sem_far.at[level - 1, i], inc=1, device_id=dev(me - 2 * dz, core), device_id_type=MESH)

    def hear(level):
        for i, dz in enumerate((1, -1)):

            @pl.when(within(dz * (level + 1)))
            def _():
                pl.semaphore_wait(sem_far.at[level - 1, i], 1)

    here = lane(me)
    loads = (
        (table_h, table),
        (streams_h.at[0], streams.at[0]),
        (streams_h.at[1], streams.at[1]),
        (streams_h.at[2], streams.at[2]),
        (short_h, short_weight),
        (modes_h, modes),
        (first_h, first),
        (filter_h.at[:, here], filter_cols),
        (decay_h.at[:, here], decay),
        (skip_h.at[:, here], skip),
        (w_h, w_out),
    )

    def load(i):
        return pltpu.make_async_copy(loads[i][0], loads[i][1], sem_in.at[i])

    for i in range(len(loads)):
        load(i).start()
    inner = jnp.logical_and(within(1), within(-1))
    pl.when(inner)(lambda: pl.semaphore_wait(barrier, 12))
    pl.when(jnp.logical_not(inner))(lambda: pl.semaphore_wait(barrier, 8))
    tell(1)
    part_rows = w_out.shape[0] // 2
    step_rows = part_rows // CHUNKS
    beside = dev(me + 1 - 2 * x, core)
    above = dev(me + 2 - 4 * (z % 2), core)
    across = (1 - grp, me, core)
    w_source = (w_h, w_h, w_next.at[1], w_next.at[0], w_next.at[1], w_next.at[2])
    w_slot = (0, 1, 2, 0, 1, 2)
    w_to = (beside, above, beside, across, across, across)

    def chunk(side_y, k):
        return pl.ds(pl.multiple_of(side_y * part_rows + k * step_rows, step_rows), step_rows)

    def w_copy(i, k):
        return pltpu.make_async_remote_copy(
            src_ref=w_source[i].at[chunk(grp, k), :], dst_ref=w_next.at[w_slot[i], chunk(grp, k), :],
            send_sem=sem_w_s.at[i, k], recv_sem=sem_w_r.at[i, k], device_id=w_to[i], device_id_type=MESH)

    def w_back(slot, k):
        return pltpu.make_async_remote_copy(
            src_ref=w_next.at[slot, chunk(1 - grp, k), :], dst_ref=w_next.at[slot, chunk(1 - grp, k), :],
            send_sem=sem_w_s.at[3 + slot, k], recv_sem=sem_w_r.at[3 + slot, k], device_id=across, device_id_type=MESH)

    def forward(i, k):
        w_copy(i, k).wait_recv()
        for nxt in ((3,), (4, 2), (5,))[i]:
            w_copy(nxt, k).start()

    def w_steps(*names):
        for name in names:
            i, k = "xzdXZD".index(name[0]), int(name[1:])
            if i < 3:
                w_copy(i, k).start()
            else:
                forward(i - 3, k)

    w_steps(*PLAN["near"])
    load(0).wait()
    eye = table[4 * blk + 2 * blk + blk : 4 * blk + 2 * blk + 2 * blk, :blk]
    for st in range(3):
        load(1 + st).wait()
        turned = lax.dot_general(eye, streams[st], (((1,), (1,)), ((), ())), preferred_element_type=f32)
        xt[st, 8:, :] = turned
    rim_out[...] = jnp.concatenate([xt[st, blk:, :] for st in range(3)], axis=0).astype(bf16)

    def features(rows):
        def body(l, carry):
            ln = lane(l)
            for r0 in rows:
                feat = []
                for st in range(3):
                    total_f = short_weight[st, pl.ds(0, 1), ln] * xt[st, pl.ds(8 + r0, 16), ln]
                    for i in range(1, taps):
                        total_f = total_f + short_weight[st, pl.ds(i, 1), ln] * xt[st, pl.ds(8 + r0 - i, 16), ln]
                    feat.append(total_f)
                q_own[pl.ds(r0, 16), ln] = feat[0].astype(bf16)
                kv_own[pl.ds(r0, 16), ln] = (feat[1] * feat[2]).astype(bf16)
            return carry

        lax.fori_loop(0, seq_count, body, 0)

    load(4).wait()
    if LATE:
        features(range(16, blk, 16))

    def rim_copy():
        return pltpu.make_async_remote_copy(
            src_ref=rim_out, dst_ref=rim_in, send_sem=sem_rim.at[0], recv_sem=sem_rim.at[1],
            device_id=dev((me + 1) % seq_count, core), device_id_type=MESH)

    def spread(own, every, send, recv, d, rows):
        to = (me + d) % seq_count
        return pltpu.make_async_remote_copy(
            src_ref=own.at[rows, lane(to)], dst_ref=every.at[rows, lane(me)],
            send_sem=send.at[d], recv_sem=recv.at[d], device_id=dev(to, core), device_id_type=MESH)

    def landing(own, every, send, recv, d, rows):
        source = (me + seq_count - d) % seq_count
        return pltpu.make_async_remote_copy(
            src_ref=own.at[rows, lane(source)], dst_ref=every.at[rows, lane(source)],
            send_sem=send.at[d], recv_sem=recv.at[d], device_id=dev(source, core), device_id_type=MESH)

    main, top, whole = pl.ds(16, blk - 16), pl.ds(0, 16), pl.ds(0, blk)
    order = (4, 3, 5, 2, 6, 1, 7) if seq_count == 8 else tuple(range(1, seq_count))

    if not LATE:
        features(range(16, blk, 16))

    hear(1)
    tell(2)

    @pl.when(me < seq_count - 1)
    def _():
        rim_copy().start()

    def reach(dz):
        for to in (z + dz) * 2 + 1 - x, (z + dz) * 2 + x:
            spread(kv_own, kv_all, sem_kvm_s, sem_kvm_r, (to + seq_count - me) % seq_count, main).start()

    spread(kv_own, kv_all, sem_kvm_s, sem_kvm_r, (seq_count + 1 - 2 * x) % seq_count, main).start()
    for span in range(1, zn):
        if span > 2:
            hear(span - 1)
            if span < zn - 1:
                tell(span)
        for dz in (span, -span):
            pl.when(within(dz))(functools.partial(reach, dz))
        if span == 1:
            w_steps(*PLAN["mid"])
    w_steps(*PLAN["kv"])

    load(5).wait()
    bands = modes.shape[0]
    band = lax.broadcasted_iota(jnp.int32, (bands, LANES), 0)
    mode = jnp.zeros((bands, LANES), jnp.int32)
    for b in range(bands):
        mode = jnp.where(band == b, modes[b], mode)
    mode = jnp.concatenate([mode] * (total // LANES), axis=1)
    steps = lax.broadcasted_iota(jnp.int32, (bands, total), 1)
    phase = (mode * steps) & (total - 1)
    turn_unit = f32(2.0 * math.pi / total)
    positional = sine(jnp.concatenate([phase + total // 4, phase], axis=0).astype(f32) * turn_unit)
    load(6).wait()
    hidden = sine(lax.dot_general(
        first[...], positional, (((0,), (0,)), ((), ())), precision=lax.Precision.HIGHEST,
        preferred_element_type=f32))
    load(7).wait()
    raw = lax.dot_general(
        hidden, filter_cols[...], (((0,), (0,)), ((), ())), precision=lax.Precision.HIGHEST,
        preferred_element_type=f32)
    load(8).wait()
    rate = decay[...]
    root = jnp.sqrt(2.0 * rate)
    pieces = []
    for r in range(seq_count):
        time = (lax.broadcasted_iota(jnp.int32, (blk, LANES), 0) + r * blk).astype(f32)
        pieces.append((root * jnp.exp(-rate * time) * raw[r * blk : (r + 1) * blk]).astype(bf16))
    now = jnp.concatenate(pieces, axis=1)
    before = jnp.concatenate([jnp.zeros((blk, LANES), bf16)] + pieces[:-1], axis=1)
    window = jnp.concatenate([before, now], axis=0)
    spectrum = jnp.dot(table[:size, :], window, preferred_element_type=f32) + jnp.dot(
        table[size : 2 * size, :], window, preferred_element_type=f32)
    row0 = lax.broadcasted_iota(jnp.int32, (blk, total), 0) == 0
    real, imag = spectrum[:blk], spectrum[blk:]
    spec_r[...] = real
    spec_i[...] = jnp.where(row0, 0.0, imag)
    spec_n[...] = jnp.where(row0, imag, real)

    @pl.when(me > 0)
    def _():
        rim_copy().wait_recv()
        for st in range(3):
            xt[st, 0:8, :] = rim_in[8 * st : 8 * st + 8, :].astype(f32)

    @pl.when(me == 0)
    def _():
        for st in range(3):
            xt[st, 0:8, :] = jnp.zeros((8, xt.shape[2]), f32)

    features((0,))
    for d in order:
        spread(kv_own, kv_all, sem_kvh_s, sem_kvh_r, d, top).start()
    w_steps(*PLAN["top"])
    for i, d in enumerate(order):
        if i >= QLAG:
            spread(kv_own, kv_all, sem_kvm_s, sem_kvm_r, order[i - QLAG], main).wait_send()
        spread(q_own, q_all, sem_q_s, sem_q_r, d, whole).start()
        w_steps(*PLAN["q"][i])
    kv_all[:, lane(me)] = kv_own[:, lane(me)]
    q_all[:, lane(me)] = q_own[:, lane(me)]

    for d in order:
        landing(kv_own, kv_all, sem_kvm_s, sem_kvm_r, d, main).wait_recv()
    for d in order:
        landing(kv_own, kv_all, sem_kvh_s, sem_kvh_r, d, top).wait_recv()
    w_steps(*PLAN["land"])
    kv = kv_all[...]
    spec_x[...] = jnp.dot(
        table[2 * size : 3 * size, :], jnp.concatenate([kv, kv], axis=0), preferred_element_type=f32)

    def product(i, carry):
        lo = pl.ds(pl.multiple_of(i * 16, 16), 16)
        hi = pl.ds(pl.multiple_of(blk + i * 16, 16), 16)
        for p in range(seq_count):
            y_real = y_imag = None
            for s in range(p + 1):
                sl, fl = pl.ds(s * LANES, LANES), pl.ds((p - s) * LANES, LANES)
                xr, xi = spec_x[lo, sl], spec_x[hi, sl]
                hr, him, hn = spec_r[lo, fl], spec_i[lo, fl], spec_n[lo, fl]
                tr = xr * hr - xi * him
                ti = xr * him + xi * hn
                y_real = tr if y_real is None else y_real + tr
                y_imag = ti if y_imag is None else y_imag + ti
            spec_y[lo, pl.ds(p * LANES, LANES)] = y_real.astype(bf16)
            spec_y[hi, pl.ds(p * LANES, LANES)] = y_imag.astype(bf16)
        return carry

    lax.fori_loop(0, blk // 16, product, 0)
    spec_r[...] = jnp.dot(table[3 * size : 3 * size + blk, :], spec_y[...], preferred_element_type=f32)
    w_steps(*PLAN["conv"])
    def rows_of(j):
        return pl.ds(pl.multiple_of(j * blk, blk), blk)

    def g_send(turn, d):
        to = (me + d) % seq_count
        far = to // groups
        rows = rows_of(1 - far if turn == 0 else far)
        return pltpu.make_async_remote_copy(
            src_ref=gate_own.at[to % groups, rows, :], dst_ref=gate_all.at[z, rows, lane(x)],
            send_sem=sem_g_s.at[turn, d], recv_sem=sem_g_r.at[turn, d], device_id=dev(to, core), device_id_type=MESH)

    def g_land(turn, d):
        source = (me + seq_count - d) % seq_count
        rows = rows_of(1 - side if turn == 0 else side)
        return pltpu.make_async_remote_copy(
            src_ref=gate_own.at[0, rows, :], dst_ref=gate_all.at[source // 2, rows, lane(source % 2)],
            send_sem=sem_g_s.at[turn, d], recv_sem=sem_g_r.at[turn, d], device_id=dev(source, core),
            device_id_type=MESH)

    load(9).wait()
    gain = skip[...]
    def apart(block):
        return (me + seq_count - block) % seq_count

    turns = [(group + i) % groups for i in range(groups)]
    own_half = [side * groups + i for i in turns]
    far_half = [(1 - side) * groups + i for i in turns]
    for i, p in enumerate(own_half + far_half):
        w_steps(*PLAN["gate"][i])
        if i:
            landing(q_own, q_all, sem_q_s, sem_q_r, apart(p), whole).wait_recv()
        sl = lane(p)
        inner = spec_r[:, sl].astype(bf16).astype(f32) + gain * kv_all[:, sl].astype(f32)
        gate_own[p % groups, rows_of(p // groups), :] = (q_all[:, sl].astype(f32) * inner).astype(bf16)
        if i != groups:
            g_send(0, (p + groups + seq_count - me) % seq_count).start()
        if i >= groups and EAGER:
            g_send(1, (p + seq_count - me) % seq_count).start()
    w_steps(*PLAN["g0"])
    for i, p in enumerate(far_half + own_half[1:]):
        if i >= groups or not EAGER:
            g_send(1, (p + seq_count - me) % seq_count).start()
        w_steps(*PLAN["g1"][i])
    gate_all[z, :, lane(x)] = gate_own[group]
    load(10).wait()

    flip_x, flip_z = 1 - 2 * x, 2 - 4 * (z % 2)
    places = (group, group + flip_z, group + flip_x, group + flip_x + flip_z)
    slots = (None, 1, 0, 2)

    def project(j, first_turn, then):
        left = [gate_all[k, rows_of(j), :] for k in range(zn)]
        for i, (place, slot) in enumerate(zip(places, slots)):
            if first_turn:
                w_steps(*PLAN["far"][i])
            if slot is not None and first_turn:
                for k in range(CHUNKS):
                    w_back(slot, k).wait_recv()
            value = None
            for k in range(zn):
                deep = pl.ds(k * 2 * LANES, 2 * LANES)
                right = w_out[deep, :] if slot is None else w_next[slot, deep, :]
                term = jnp.dot(left[k], right, preferred_element_type=f32)
                value = term if value is None else value + term
            acc[rows_of(j), lane(place, cols)] = value
            then(place)

    def a_copy(i):
        return pltpu.make_async_remote_copy(
            src_ref=acc.at[rows_of(other), lane(i, cols)], dst_ref=acc_in.at[:, lane(i, cols)],
            send_sem=sem_a_s.at[i], recv_sem=sem_a_r.at[i], device_id=dev(me, other), device_id_type=MESH)

    def o_copy(i):
        return pltpu.make_async_remote_copy(
            src_ref=part.at[:, lane(i, cols)], dst_ref=out.at[:, lane(i, cols)],
            send_sem=sem_o_s.at[i], recv_sem=sem_o_r.at[i], device_id=dev(groups * core + group, side),
            device_id_type=MESH)

    for d in order:
        g_land(0, d).wait_recv()
    def give(place):
        a_copy(place).start()

    def take(place, store):
        a_copy(place).wait_recv()
        ln = lane(place, cols)
        store[:, ln] = (acc[rows_of(core), ln] + acc_in[:, ln]).astype(bf16)

    def far(place):
        pl.when(core == side)(lambda: give(place))

        @pl.when(core != side)
        def _():
            take(place, part)
            o_copy(place).start()

    def near(place):
        pl.when(core != side)(lambda: give(place))
        pl.when(core == side)(lambda: take(place, out))

    project(1 - side, True, far)
    for d in order:
        g_land(1, d).wait_recv()
    project(side, False, near)

    @pl.when(core != side)
    def _():
        for i in range(groups):
            o_copy(i).wait_recv()
            o_copy(i).wait_send()

    @pl.when(me < seq_count - 1)
    def _():
        rim_copy().wait_send()

    for d in order:
        spread(kv_own, kv_all, sem_kvh_s, sem_kvh_r, d, top).wait_send()
        spread(q_own, q_all, sem_q_s, sem_q_r, d, whole).wait_send()
        g_send(0, d).wait_send()
        g_send(1, d).wait_send()
    for d in order[max(0, len(order) - QLAG) :]:
        spread(kv_own, kv_all, sem_kvm_s, sem_kvm_r, d, main).wait_send()
    for i in range(6):
        for k in range(CHUNKS):
            w_copy(i, k).wait_send()
    for i in range(groups):
        a_copy(i).wait_send()


def fused(
    streams, short_weight, filter_modes, filter_first, filter_out, decay_rate, skip_gain, w_out
):
    f32, bf16 = jnp.float32, jnp.bfloat16
    n = lax.axis_size("seq")
    width, blk = streams.shape[1], streams.shape[2]
    cols = w_out.shape[1]
    total = n * blk
    dma = pltpu.SemaphoreType.DMA
    vmem = pltpu.VMEM
    return pl.pallas_call(
        functools.partial(mixer, n),
        out_shape=pltpu.VMEM((blk, n * cols // 2), bf16),
        in_specs=[
            pl.BlockSpec(memory_space=pltpu.HBM) for _ in range(9)
        ],
        out_specs=pl.BlockSpec(memory_space=pltpu.VMEM),
        scratch_shapes=[
            vmem(streams.shape, bf16),
            vmem(short_weight.shape, f32),
            pltpu.SMEM(filter_modes.shape, jnp.int32),
            vmem(filter_first.shape, f32),
            vmem((filter_out.shape[0], LANES), f32),
            vmem((1, LANES), f32),
            vmem((1, LANES), f32),
            vmem(w_out.shape, bf16),
            vmem((8 * blk, 2 * blk), bf16),
            vmem((3, 8 + blk, width), f32),
            vmem((24, width), bf16),
            vmem((24, width), bf16),
            vmem((blk, width), bf16),
            vmem((blk, width), bf16),
            vmem((blk, total), bf16),
            vmem((blk, total), bf16),
            vmem((2 * blk, total), f32),
            vmem((blk, total), f32),
            vmem((blk, total), f32),
            vmem((blk, total), f32),
            vmem((2 * blk, total), bf16),
            vmem((n // 2, 2 * blk, LANES), bf16),
            vmem((n // 2, 2 * blk, 2 * LANES), bf16),
            vmem((3, *w_out.shape), bf16),
            vmem((2 * blk, n // 2 * cols), f32),
            vmem((blk, n // 2 * cols), f32),
            vmem((blk, n // 2 * cols), bf16),
            pltpu.SemaphoreType.REGULAR((2, 2)),
            dma((11,)),
            dma((2,)),
            dma((n,)), dma((n,)),
            dma((n,)), dma((n,)),
            dma((n,)), dma((n,)),
            dma((2, n)), dma((2, n)),
            dma((6, CHUNKS)), dma((6, CHUNKS)),
            dma((n // 2,)), dma((n // 2,)),
            dma((n // 2,)), dma((n // 2,)),
        ],
        compiler_params=pltpu.CompilerParams(
            collective_id=0, has_side_effects=True, vmem_limit_bytes=56 * 1024 * 1024
        ),
    )(
        streams, short_weight, filter_modes, filter_first, filter_out,
        decay_rate.reshape(1, -1), skip_gain.reshape(1, -1), w_out, jnp.asarray(tables(blk)),
    )


def plan(
    streams, short_weight, filter_modes, filter_first, filter_out, decay_rate, skip_gain, w_out
):
    n = lax.axis_size("seq")
    width, blk = streams.shape[1], streams.shape[2]
    fits = n == 8 and lax.axis_size("chan") == 2 and lax.axis_size("grp") == 2 and blk == LANES and width == n * LANES
    fits = fits and short_weight.shape[1] <= 9 and w_out.shape[1] % LANES == 0
    form = fused if fits else local
    return form(
        streams, short_weight, filter_modes, filter_first, filter_out, decay_rate, skip_gain, w_out
    )


def solution(mesh):
    return jax.shard_map(
        plan,
        mesh=mesh,
        in_specs=(
            P(None, "chan", ("grp", "seq")),
            P(None, None, "chan"),
            P(),
            P(),
            P(None, "chan"),
            P("chan"),
            P("chan"),
            P("chan", "seq"),
        ),
        out_specs=P(("grp", "seq"), "chan"),
        check_vma=False,
    )
```

```python
import functools
import math

import jax
import jax.numpy as jnp
import numpy as np
from jax import lax
from jax.experimental import pallas as pl
from jax.experimental.pallas import tpu as pltpu
from jax.sharding import PartitionSpec as P


def shifted(value, axis, steps):
    count = lax.axis_size(axis)
    leading, last = (max(0, -steps), min(count, count - steps))
    return lax.ppermute(value, axis, [(source, source + steps) for source in range(leading, last)])


def position_filter(
    positions, mode_ints, first_layer, out_cols, decay_rates, tokens_dev, seq_count
):
    total_len = tokens_dev * seq_count
    block_idx = positions // tokens_dev
    offset_idx = positions % tokens_dev
    upper_part = mode_ints[:, None] * block_idx[None, :] % seq_count
    lower_part = mode_ints[:, None] * offset_idx[None, :] % total_len
    phase_int = (tokens_dev * upper_part + lower_part) % total_len
    phase_angle = phase_int.astype(jnp.float32) * jnp.float32(2.0 * math.pi / total_len)
    features = jnp.concatenate([jnp.cos(phase_angle), jnp.sin(phase_angle)], axis=0)
    hidden = jnp.sin(
        jnp.dot(
            first_layer.T,
            features,
            precision=lax.Precision.HIGHEST,
            preferred_element_type=jnp.float32,
        )
    )
    raw_values = jnp.dot(
        out_cols.T, hidden, precision=lax.Precision.HIGHEST, preferred_element_type=jnp.float32
    )
    time_float = positions.astype(jnp.float32)
    scaled = (
        jnp.sqrt(2.0 * decay_rates)[:, None]
        * jnp.exp(-decay_rates[:, None] * time_float[None, :])
        * raw_values
    )
    return scaled.astype(jnp.bfloat16)


def angle_table(rows_count, cols_count, modulus):
    product = (
        jnp.arange(rows_count, dtype=jnp.int32)[:, None]
        * jnp.arange(cols_count, dtype=jnp.int32)[None, :]
        % modulus
    )
    phase_angle = product.astype(jnp.float32) * jnp.float32(2.0 * math.pi / modulus)
    return (jnp.cos(phase_angle), jnp.sin(phase_angle))


def contract(form, left, right):
    return jnp.einsum(
        form, left, right, precision=lax.Precision.HIGHEST, preferred_element_type=jnp.float32
    )


def local(
    streams, short_weight, filter_modes, filter_first, filter_out, decay_rate, skip_gain, w_out
):
    seq_count = lax.axis_size("seq")
    seq_index = lax.axis_index("seq")
    width_half = streams.shape[1]
    tokens_dev = streams.shape[2]
    reach = short_weight.shape[1] - 1
    per_device = width_half // seq_count
    total_len = tokens_dev * seq_count
    rim = shifted(streams[:, :, tokens_dev - reach :], "seq", 1)
    extended = jnp.concatenate([rim, streams], axis=2).astype(jnp.float32)
    feature = short_weight[:, 0, :, None] * extended[:, :, reach:]
    for tap_index in range(1, reach + 1):
        feature = (
            feature
            + short_weight[:, tap_index, :, None]
            * extended[:, :, reach - tap_index : reach - tap_index + tokens_dev]
        )
    query = feature[0].astype(jnp.bfloat16)
    kv_product = (feature[1] * feature[2]).astype(jnp.bfloat16)
    positions = seq_index * tokens_dev + jnp.arange(tokens_dev, dtype=jnp.int32)
    filter_local = position_filter(
        positions, filter_modes, filter_first, filter_out, decay_rate, tokens_dev, seq_count
    )
    kv_channels, filter_channels = (
        lax.all_to_all(kv_product, "seq", split_axis=0, concat_axis=1, tiled=True),
        lax.all_to_all(filter_local, "seq", split_axis=0, concat_axis=1, tiled=True),
    )
    doubled = 2 * seq_count
    padded_len = 2 * total_len
    cos_outer, sin_outer = angle_table(doubled, seq_count, doubled)
    cos_twist, sin_twist = angle_table(doubled, tokens_dev, padded_len)
    cos_inner, sin_inner = angle_table(tokens_dev, tokens_dev, tokens_dev)

    def forward(signal):
        shaped = signal.astype(jnp.float32).reshape(per_device, seq_count, tokens_dev)
        a_real = contract("cpj,kp->ckj", shaped, cos_outer)
        a_imag = -contract("cpj,kp->ckj", shaped, sin_outer)
        r_real = a_real * cos_twist + a_imag * sin_twist
        r_imag = a_imag * cos_twist - a_real * sin_twist
        x_real = contract("ckj,jm->ckm", r_real, cos_inner) + contract(
            "ckj,jm->ckm", r_imag, sin_inner
        )
        x_imag = contract("ckj,jm->ckm", r_imag, cos_inner) - contract(
            "ckj,jm->ckm", r_real, sin_inner
        )
        return (x_real, x_imag)

    kv_real, kv_imag = forward(kv_channels)
    fl_real, fl_imag = forward(filter_channels)
    y_real = kv_real * fl_real - kv_imag * fl_imag
    y_imag = kv_real * fl_imag + kv_imag * fl_real
    b_real = contract("ckm,mj->ckj", y_real, cos_inner) - contract("ckm,mj->ckj", y_imag, sin_inner)
    b_imag = contract("ckm,mj->ckj", y_imag, cos_inner) + contract("ckm,mj->ckj", y_real, sin_inner)
    t_real = b_real * cos_twist - b_imag * sin_twist
    t_imag = b_real * sin_twist + b_imag * cos_twist
    conv_values = contract("ckj,kp->cpj", t_real, cos_outer) - contract(
        "ckj,kp->cpj", t_imag, sin_outer
    )
    conv_channels = (
        (conv_values * jnp.float32(1.0 / padded_len))
        .reshape(per_device, total_len)
        .astype(jnp.bfloat16)
    )
    conv_tokens = lax.all_to_all(conv_channels, "seq", split_axis=1, concat_axis=0, tiled=True)
    gated = (
        query.astype(jnp.float32)
        * (conv_tokens.astype(jnp.float32) + skip_gain[:, None] * kv_product.astype(jnp.float32))
    ).astype(jnp.bfloat16)
    partial_out = lax.dot_general(
        gated,
        lax.all_gather(w_out, "seq", axis=1, tiled=True),
        (((0,), (0,)), ((), ())),
        preferred_element_type=jnp.float32,
    )
    return lax.psum_scatter(partial_out, "chan", scatter_dimension=1, tiled=True).astype(
        jnp.bfloat16
    )


LANES = 128
CHUNKS = 4
QLAG = 7
LATE = False
EAGER = True
PLAN = {'near': ('z0', 'x0', 'z1', 'x1'), 'mid': (), 'kv': ('x2', 'x3'), 'top': (), 'q': ((), (), (), (), (), (), ('z2', 'z3', 'X0', 'Z0', 'X1', 'Z1', 'X2')), 'land': (), 'conv': ('Z2', 'X3'), 'gate': ((), (), (), (), (), (), (), ()), 'g0': (), 'g1': ((), (), (), (), (), (), ('D0', 'Z3', 'D1', 'D2', 'D3')), 'far': ((), (), (), ())}
MESH = pl.DeviceIdType.MESH


def tables(block):
    size = 2 * block
    steps = np.arange(size)
    angle = 2.0 * np.pi * (np.outer(np.arange(block), steps) % size) / size
    forward = np.concatenate([np.cos(angle), -np.sin(angle)], axis=0)
    forward[block] = np.cos(np.pi * steps)
    weight = np.full((size, 1), 2.0 / size)
    weight[0] = weight[block] = 1.0 / size
    inverse = (forward * weight).T[block:]
    upper = np.asarray(forward, dtype=jnp.bfloat16)
    lower = np.asarray(forward - upper.astype(np.float64), dtype=jnp.bfloat16)
    both = np.concatenate([upper[:, :block], lower[:, :block]], axis=1)
    unit = np.eye(block, size)
    return np.concatenate(
        [upper, lower, both, np.asarray(inverse, jnp.bfloat16), np.asarray(unit, jnp.bfloat16)], axis=0
    )


def split_pi():
    parts, rest = [], math.pi
    for bits in (10, 22):
        part = math.floor(rest * 2.0**bits) / 2.0**bits
        parts.append(part)
        rest -= part
    return (*parts, rest)


def sine(value):
    f32 = jnp.float32
    count = jnp.floor(value * f32(1.0 / math.pi) + f32(0.5))
    rest = value
    for part in split_pi():
        rest = rest - count * f32(part)
    half = count * f32(0.5)
    sign = f32(1.0) - f32(4.0) * (half - jnp.floor(half))
    square = rest * rest
    series = f32(0.0)
    for degree in range(13, 1, -2):
        series = (series + f32((-1.0) ** (degree // 2) / math.factorial(degree))) * square
    return sign * (rest + rest * series)


def mixer(
    seq_count, streams_h, short_h, modes_h, first_h, filter_h, decay_h, skip_h, w_h, table_h, out,
    streams, short_weight, modes, first, filter_cols, decay, skip, w_out, table,
    xt, rim_out, rim_in, kv_own, q_own, kv_all, q_all, spec_x, spec_r, spec_i, spec_n, spec_y,
    gate_own, gate_all, w_next, acc, acc_in, part,
    sem_far, sem_in, sem_rim, sem_kvm_s, sem_kvm_r, sem_kvh_s, sem_kvh_r, sem_q_s, sem_q_r, sem_g_s, sem_g_r,
    sem_w_s, sem_w_r, sem_a_s, sem_a_r, sem_o_s, sem_o_r,
):
    f32, bf16 = jnp.float32, jnp.bfloat16
    blk = streams.shape[2]
    size = 2 * blk
    taps = short_weight.shape[1]
    total = seq_count * blk
    cols = w_out.shape[1]
    zn = seq_count // 2
    groups = seq_count // 2
    grp = lax.axis_index("grp")
    me = lax.axis_index("seq")
    core = lax.axis_index("chan")
    other = 1 - core
    z = me // 2
    x = me % 2
    side = me // groups
    group = me % groups

    def dev(seq, chan):
        return (grp, seq, chan)

    def lane(i, n=LANES):
        return pl.ds(pl.multiple_of(i * n, n), n)

    barrier = pltpu.get_barrier_semaphore()
    def within(dz):
        return jnp.logical_and(z + dz >= 0, z + dz < zn)

    def hello(to):
        pl.semaphore_signal(barrier, inc=1, device_id=to, device_id_type=MESH)

    for dz in (1, -1):

        @pl.when(within(dz))
        def _():
            for px in range(2):
                for ch in (core, other):
                    hello(dev((z + dz) * 2 + px, ch))

    for near in (dev(z * 2 + 1 - x, core), dev(z * 2 + 1 - x, other), dev(me, other), (1 - grp, me, core)):
        hello(near)

    def tell(level):
        for i, dz in enumerate((1, -1)):

            @pl.when(jnp.logical_and(within(-dz), within(dz * level)))
            def _():
                pl.semaphore_signal(
                    sem_far.at[level - 1, i], inc=1, device_id=dev(me - 2 * dz, core), device_id_type=MESH)

    def hear(level):
        for i, dz in enumerate((1, -1)):

            @pl.when(within(dz * (level + 1)))
            def _():
                pl.semaphore_wait(sem_far.at[level - 1, i], 1)

    here = lane(me)
    loads = (
        (table_h, table),
        (streams_h.at[0], streams.at[0]),
        (streams_h.at[1], streams.at[1]),
        (streams_h.at[2], streams.at[2]),
        (short_h, short_weight),
        (modes_h, modes),
        (first_h, first),
        (filter_h.at[:, here], filter_cols),
        (decay_h.at[:, here], decay),
        (skip_h.at[:, here], skip),
        (w_h, w_out),
    )

    def load(i):
        return pltpu.make_async_copy(loads[i][0], loads[i][1], sem_in.at[i])

    for i in range(len(loads)):
        load(i).start()
    inner = jnp.logical_and(within(1), within(-1))
    pl.when(inner)(lambda: pl.semaphore_wait(barrier, 12))
    pl.when(jnp.logical_not(inner))(lambda: pl.semaphore_wait(barrier, 8))
    tell(1)
    part_rows = w_out.shape[0] // 2
    step_rows = part_rows // CHUNKS
    beside = dev(me + 1 - 2 * x, core)
    above = dev(me + 2 - 4 * (z % 2), core)
    across = (1 - grp, me, core)
    w_source = (w_h, w_h, w_next.at[1], w_next.at[0], w_next.at[1], w_next.at[2])
    w_slot = (0, 1, 2, 0, 1, 2)
    w_to = (beside, above, beside, across, across, across)

    def chunk(side_y, k):
        return pl.ds(pl.multiple_of(side_y * part_rows + k * step_rows, step_rows), step_rows)

    def w_copy(i, k):
        return pltpu.make_async_remote_copy(
            src_ref=w_source[i].at[chunk(grp, k), :], dst_ref=w_next.at[w_slot[i], chunk(grp, k), :],
            send_sem=sem_w_s.at[i, k], recv_sem=sem_w_r.at[i, k], device_id=w_to[i], device_id_type=MESH)

    def w_back(slot, k):
        return pltpu.make_async_remote_copy(
            src_ref=w_next.at[slot, chunk(1 - grp, k), :], dst_ref=w_next.at[slot, chunk(1 - grp, k), :],
            send_sem=sem_w_s.at[3 + slot, k], recv_sem=sem_w_r.at[3 + slot, k], device_id=across, device_id_type=MESH)

    def forward(i, k):
        w_copy(i, k).wait_recv()
        for nxt in ((3,), (4, 2), (5,))[i]:
            w_copy(nxt, k).start()

    def w_steps(*names):
        for name in names:
            i, k = "xzdXZD".index(name[0]), int(name[1:])
            if i < 3:
                w_copy(i, k).start()
            else:
                forward(i - 3, k)

    w_steps(*PLAN["near"])
    load(0).wait()
    eye = table[4 * blk + 2 * blk + blk : 4 * blk + 2 * blk + 2 * blk, :blk]
    for st in range(3):
        load(1 + st).wait()
        turned = lax.dot_general(eye, streams[st], (((1,), (1,)), ((), ())), preferred_element_type=f32)
        xt[st, 8:, :] = turned
    rim_out[...] = jnp.concatenate([xt[st, blk:, :] for st in range(3)], axis=0).astype(bf16)

    def features(rows):
        def body(l, carry):
            ln = lane(l)
            for r0 in rows:
                feat = []
                for st in range(3):
                    total_f = short_weight[st, pl.ds(0, 1), ln] * xt[st, pl.ds(8 + r0, 16), ln]
                    for i in range(1, taps):
                        total_f = total_f + short_weight[st, pl.ds(i, 1), ln] * xt[st, pl.ds(8 + r0 - i, 16), ln]
                    feat.append(total_f)
                q_own[pl.ds(r0, 16), ln] = feat[0].astype(bf16)
                kv_own[pl.ds(r0, 16), ln] = (feat[1] * feat[2]).astype(bf16)
            return carry

        lax.fori_loop(0, seq_count, body, 0)

    load(4).wait()
    if LATE:
        features(range(16, blk, 16))

    def rim_copy():
        return pltpu.make_async_remote_copy(
            src_ref=rim_out, dst_ref=rim_in, send_sem=sem_rim.at[0], recv_sem=sem_rim.at[1],
            device_id=dev((me + 1) % seq_count, core), device_id_type=MESH)

    def spread(own, every, send, recv, d, rows):
        to = (me + d) % seq_count
        return pltpu.make_async_remote_copy(
            src_ref=own.at[rows, lane(to)], dst_ref=every.at[rows, lane(me)],
            send_sem=send.at[d], recv_sem=recv.at[d], device_id=dev(to, core), device_id_type=MESH)

    def landing(own, every, send, recv, d, rows):
        source = (me + seq_count - d) % seq_count
        return pltpu.make_async_remote_copy(
            src_ref=own.at[rows, lane(source)], dst_ref=every.at[rows, lane(source)],
            send_sem=send.at[d], recv_sem=recv.at[d], device_id=dev(source, core), device_id_type=MESH)

    main, top, whole = pl.ds(16, blk - 16), pl.ds(0, 16), pl.ds(0, blk)
    order = (4, 3, 5, 2, 6, 1, 7) if seq_count == 8 else tuple(range(1, seq_count))

    if not LATE:
        features(range(16, blk, 16))

    hear(1)
    tell(2)

    @pl.when(me < seq_count - 1)
    def _():
        rim_copy().start()

    def reach(dz):
        for to in (z + dz) * 2 + 1 - x, (z + dz) * 2 + x:
            spread(kv_own, kv_all, sem_kvm_s, sem_kvm_r, (to + seq_count - me) % seq_count, main).start()

    spread(kv_own, kv_all, sem_kvm_s, sem_kvm_r, (seq_count + 1 - 2 * x) % seq_count, main).start()
    for span in range(1, zn):
        if span > 2:
            hear(span - 1)
            if span < zn - 1:
                tell(span)
        for dz in (span, -span):
            pl.when(within(dz))(functools.partial(reach, dz))
        if span == 1:
            w_steps(*PLAN["mid"])
    w_steps(*PLAN["kv"])

    load(5).wait()
    bands = modes.shape[0]
    band = lax.broadcasted_iota(jnp.int32, (bands, LANES), 0)
    mode = jnp.zeros((bands, LANES), jnp.int32)
    for b in range(bands):
        mode = jnp.where(band == b, modes[b], mode)
    mode = jnp.concatenate([mode] * (total // LANES), axis=1)
    steps = lax.broadcasted_iota(jnp.int32, (bands, total), 1)
    phase = (mode * steps) & (total - 1)
    turn_unit = f32(2.0 * math.pi / total)
    positional = sine(jnp.concatenate([phase + total // 4, phase], axis=0).astype(f32) * turn_unit)
    load(6).wait()
    hidden = sine(lax.dot_general(
        first[...], positional, (((0,), (0,)), ((), ())), precision=lax.Precision.HIGHEST,
        preferred_element_type=f32))
    load(7).wait()
    raw = lax.dot_general(
        hidden, filter_cols[...], (((0,), (0,)), ((), ())), precision=lax.Precision.HIGHEST,
        preferred_element_type=f32)
    load(8).wait()
    rate = decay[...]
    root = jnp.sqrt(2.0 * rate)
    pieces = []
    for r in range(seq_count):
        time = (lax.broadcasted_iota(jnp.int32, (blk, LANES), 0) + r * blk).astype(f32)
        pieces.append((root * jnp.exp(-rate * time) * raw[r * blk : (r + 1) * blk]).astype(bf16))
    now = jnp.concatenate(pieces, axis=1)
    before = jnp.concatenate([jnp.zeros((blk, LANES), bf16)] + pieces[:-1], axis=1)
    window = jnp.concatenate([before, now], axis=0)
    spectrum = jnp.dot(table[:size, :], window, preferred_element_type=f32) + jnp.dot(
        table[size : 2 * size, :], window, preferred_element_type=f32)
    row0 = lax.broadcasted_iota(jnp.int32, (blk, total), 0) == 0
    real, imag = spectrum[:blk], spectrum[blk:]
    spec_r[...] = real
    spec_i[...] = jnp.where(row0, 0.0, imag)
    spec_n[...] = jnp.where(row0, imag, real)

    @pl.when(me > 0)
    def _():
        rim_copy().wait_recv()
        for st in range(3):
            xt[st, 0:8, :] = rim_in[8 * st : 8 * st + 8, :].astype(f32)

    @pl.when(me == 0)
    def _():
        for st in range(3):
            xt[st, 0:8, :] = jnp.zeros((8, xt.shape[2]), f32)

    features((0,))
    for d in order:
        spread(kv_own, kv_all, sem_kvh_s, sem_kvh_r, d, top).start()
    w_steps(*PLAN["top"])
    for i, d in enumerate(order):
        if i >= QLAG:
            spread(kv_own, kv_all, sem_kvm_s, sem_kvm_r, order[i - QLAG], main).wait_send()
        spread(q_own, q_all, sem_q_s, sem_q_r, d, whole).start()
        w_steps(*PLAN["q"][i])
    kv_all[:, lane(me)] = kv_own[:, lane(me)]
    q_all[:, lane(me)] = q_own[:, lane(me)]

    for d in order:
        landing(kv_own, kv_all, sem_kvm_s, sem_kvm_r, d, main).wait_recv()
    for d in order:
        landing(kv_own, kv_all, sem_kvh_s, sem_kvh_r, d, top).wait_recv()
    w_steps(*PLAN["land"])
    kv = kv_all[...]
    spec_x[...] = jnp.dot(
        table[2 * size : 3 * size, :], jnp.concatenate([kv, kv], axis=0), preferred_element_type=f32)

    def product(i, carry):
        lo = pl.ds(pl.multiple_of(i * 16, 16), 16)
        hi = pl.ds(pl.multiple_of(blk + i * 16, 16), 16)
        for p in range(seq_count):
            y_real = y_imag = None
            for s in range(p + 1):
                sl, fl = pl.ds(s * LANES, LANES), pl.ds((p - s) * LANES, LANES)
                xr, xi = spec_x[lo, sl], spec_x[hi, sl]
                hr, him, hn = spec_r[lo, fl], spec_i[lo, fl], spec_n[lo, fl]
                tr = xr * hr - xi * him
                ti = xr * him + xi * hn
                y_real = tr if y_real is None else y_real + tr
                y_imag = ti if y_imag is None else y_imag + ti
            spec_y[lo, pl.ds(p * LANES, LANES)] = y_real.astype(bf16)
            spec_y[hi, pl.ds(p * LANES, LANES)] = y_imag.astype(bf16)
        return carry

    lax.fori_loop(0, blk // 16, product, 0)
    spec_r[...] = jnp.dot(table[3 * size : 3 * size + blk, :], spec_y[...], preferred_element_type=f32)
    w_steps(*PLAN["conv"])
    def rows_of(j):
        return pl.ds(pl.multiple_of(j * blk, blk), blk)

    def g_send(turn, d):
        to = (me + d) % seq_count
        far = to // groups
        rows = rows_of(1 - far if turn == 0 else far)
        return pltpu.make_async_remote_copy(
            src_ref=gate_own.at[to % groups, rows, :], dst_ref=gate_all.at[z, rows, lane(x)],
            send_sem=sem_g_s.at[turn, d], recv_sem=sem_g_r.at[turn, d], device_id=dev(to, core), device_id_type=MESH)

    def g_land(turn, d):
        source = (me + seq_count - d) % seq_count
        rows = rows_of(1 - side if turn == 0 else side)
        return pltpu.make_async_remote_copy(
            src_ref=gate_own.at[0, rows, :], dst_ref=gate_all.at[source // 2, rows, lane(source % 2)],
            send_sem=sem_g_s.at[turn, d], recv_sem=sem_g_r.at[turn, d], device_id=dev(source, core),
            device_id_type=MESH)

    load(9).wait()
    gain = skip[...]
    def apart(block):
        return (me + seq_count - block) % seq_count

    turns = [(group + i) % groups for i in range(groups)]
    own_half = [side * groups + i for i in turns]
    far_half = [(1 - side) * groups + i for i in turns]
    for i, p in enumerate(own_half + far_half):
        w_steps(*PLAN["gate"][i])
        if i:
            landing(q_own, q_all, sem_q_s, sem_q_r, apart(p), whole).wait_recv()
        sl = lane(p)
        inner = spec_r[:, sl].astype(bf16).astype(f32) + gain * kv_all[:, sl].astype(f32)
        gate_own[p % groups, rows_of(p // groups), :] = (q_all[:, sl].astype(f32) * inner).astype(bf16)
        if i != groups:
            g_send(0, (p + groups + seq_count - me) % seq_count).start()
        if i >= groups and EAGER:
            g_send(1, (p + seq_count - me) % seq_count).start()
    w_steps(*PLAN["g0"])
    for i, p in enumerate(far_half + own_half[1:]):
        if i >= groups or not EAGER:
            g_send(1, (p + seq_count - me) % seq_count).start()
        w_steps(*PLAN["g1"][i])
    gate_all[z, :, lane(x)] = gate_own[group]
    load(10).wait()

    flip_x, flip_z = 1 - 2 * x, 2 - 4 * (z % 2)
    places = (group, group + flip_z, group + flip_x, group + flip_x + flip_z)
    slots = (None, 1, 0, 2)

    def project(j, first_turn, then):
        left = [gate_all[k, rows_of(j), :] for k in range(zn)]
        for i, (place, slot) in enumerate(zip(places, slots)):
            if first_turn:
                w_steps(*PLAN["far"][i])
            if slot is not None and first_turn:
                for k in range(CHUNKS):
                    w_back(slot, k).wait_recv()
            value = None
            for k in range(zn):
                deep = pl.ds(k * 2 * LANES, 2 * LANES)
                right = w_out[deep, :] if slot is None else w_next[slot, deep, :]
                term = jnp.dot(left[k], right, preferred_element_type=f32)
                value = term if value is None else value + term
            acc[rows_of(j), lane(place, cols)] = value
            then(place)

    def a_copy(i):
        return pltpu.make_async_remote_copy(
            src_ref=acc.at[rows_of(other), lane(i, cols)], dst_ref=acc_in.at[:, lane(i, cols)],
            send_sem=sem_a_s.at[i], recv_sem=sem_a_r.at[i], device_id=dev(me, other), device_id_type=MESH)

    def o_copy(i):
        return pltpu.make_async_remote_copy(
            src_ref=part.at[:, lane(i, cols)], dst_ref=out.at[:, lane(i, cols)],
            send_sem=sem_o_s.at[i], recv_sem=sem_o_r.at[i], device_id=dev(groups * core + group, side),
            device_id_type=MESH)

    for d in order:
        g_land(0, d).wait_recv()
    def give(place):
        a_copy(place).start()

    def take(place, store):
        a_copy(place).wait_recv()
        ln = lane(place, cols)
        store[:, ln] = (acc[rows_of(core), ln] + acc_in[:, ln]).astype(bf16)

    def far(place):
        pl.when(core == side)(lambda: give(place))

        @pl.when(core != side)
        def _():
            take(place, part)
            o_copy(place).start()

    def near(place):
        pl.when(core != side)(lambda: give(place))
        pl.when(core == side)(lambda: take(place, out))

    project(1 - side, True, far)
    for d in order:
        g_land(1, d).wait_recv()
    project(side, False, near)

    @pl.when(core != side)
    def _():
        for i in range(groups):
            o_copy(i).wait_recv()
            o_copy(i).wait_send()

    @pl.when(me < seq_count - 1)
    def _():
        rim_copy().wait_send()

    for d in order:
        spread(kv_own, kv_all, sem_kvh_s, sem_kvh_r, d, top).wait_send()
        spread(q_own, q_all, sem_q_s, sem_q_r, d, whole).wait_send()
        g_send(0, d).wait_send()
        g_send(1, d).wait_send()
    for d in order[max(0, len(order) - QLAG) :]:
        spread(kv_own, kv_all, sem_kvm_s, sem_kvm_r, d, main).wait_send()
    for i in range(6):
        for k in range(CHUNKS):
            w_copy(i, k).wait_send()
    for i in range(groups):
        a_copy(i).wait_send()


def fused(
    streams, short_weight, filter_modes, filter_first, filter_out, decay_rate, skip_gain, w_out
):
    f32, bf16 = jnp.float32, jnp.bfloat16
    n = lax.axis_size("seq")
    width, blk = streams.shape[1], streams.shape[2]
    cols = w_out.shape[1]
    total = n * blk
    dma = pltpu.SemaphoreType.DMA
    vmem = pltpu.VMEM
    return pl.pallas_call(
        functools.partial(mixer, n),
        out_shape=pltpu.VMEM((blk, n * cols // 2), bf16),
        in_specs=[
            pl.BlockSpec(memory_space=pltpu.HBM) for _ in range(9)
        ],
        out_specs=pl.BlockSpec(memory_space=pltpu.VMEM),
        scratch_shapes=[
            vmem(streams.shape, bf16),
            vmem(short_weight.shape, f32),
            pltpu.SMEM(filter_modes.shape, jnp.int32),
            vmem(filter_first.shape, f32),
            vmem((filter_out.shape[0], LANES), f32),
            vmem((1, LANES), f32),
            vmem((1, LANES), f32),
            vmem(w_out.shape, bf16),
            vmem((8 * blk, 2 * blk), bf16),
            vmem((3, 8 + blk, width), f32),
            vmem((24, width), bf16),
            vmem((24, width), bf16),
            vmem((blk, width), bf16),
            vmem((blk, width), bf16),
            vmem((blk, total), bf16),
            vmem((blk, total), bf16),
            vmem((2 * blk, total), f32),
            vmem((blk, total), f32),
            vmem((blk, total), f32),
            vmem((blk, total), f32),
            vmem((2 * blk, total), bf16),
            vmem((n // 2, 2 * blk, LANES), bf16),
            vmem((n // 2, 2 * blk, 2 * LANES), bf16),
            vmem((3, *w_out.shape), bf16),
            vmem((2 * blk, n // 2 * cols), f32),
            vmem((blk, n // 2 * cols), f32),
            vmem((blk, n // 2 * cols), bf16),
            pltpu.SemaphoreType.REGULAR((2, 2)),
            dma((11,)),
            dma((2,)),
            dma((n,)), dma((n,)),
            dma((n,)), dma((n,)),
            dma((n,)), dma((n,)),
            dma((2, n)), dma((2, n)),
            dma((6, CHUNKS)), dma((6, CHUNKS)),
            dma((n // 2,)), dma((n // 2,)),
            dma((n // 2,)), dma((n // 2,)),
        ],
        compiler_params=pltpu.CompilerParams(
            collective_id=0, has_side_effects=True, vmem_limit_bytes=56 * 1024 * 1024
        ),
    )(
        streams, short_weight, filter_modes, filter_first, filter_out,
        decay_rate.reshape(1, -1), skip_gain.reshape(1, -1), w_out, jnp.asarray(tables(blk)),
    )


def plan(
    streams, short_weight, filter_modes, filter_first, filter_out, decay_rate, skip_gain, w_out
):
    n = lax.axis_size("seq")
    width, blk = streams.shape[1], streams.shape[2]
    fits = n == 8 and lax.axis_size("chan") == 2 and lax.axis_size("grp") == 2 and blk == LANES and width == n * LANES
    fits = fits and short_weight.shape[1] <= 9 and w_out.shape[1] % LANES == 0
    form = fused if fits else local
    return form(
        streams, short_weight, filter_modes, filter_first, filter_out, decay_rate, skip_gain, w_out
    )


def solution(mesh):
    return jax.shard_map(
        plan,
        mesh=mesh,
        in_specs=(
            P(None, "chan", ("grp", "seq")),
            P(None, None, "chan"),
            P(),
            P(),
            P(None, "chan"),
            P("chan"),
            P("chan"),
            P("chan", "seq"),
        ),
        out_specs=P(("grp", "seq"), "chan"),
        check_vma=False,
    )
```
